256 devices in a mesh: front: 8 (over z), row: 4 (over x_hi, core), col: 8 (over x_lo, y).
Axes of the slice: x: 4 (x_hi: 2, x_lo: 2; x = x_hi * 2 + x_lo), y: 4, z: 8, core: 2. Of those that a mesh axis runs over, the one named last changes fastest.
Arguments:
- front_slab: bfloat16 [8, 2048, 8192], P('front', 'row', 'col'), may hold values from -0.0625 to 0.0625
- samples: bfloat16 [8192, 256], P(('row', 'col')), may hold values from -6 to 6
- child_tiles: bfloat16 [512, 128, 2048], P(('front', 'row', 'col')), may hold values from -0.0625 to 0.0625
- parent_front: int32 [512, 1], P(('front', 'row', 'col')), may hold values from 0 to 7; in each aligned block of 2 rows (0 to 1, 2 to 3, ...) at most 2 rows name the same one
- parent_tile: int32 [512], P(('front', 'row', 'col')), may hold values from 0 to 15
- column_tiles: int32 [512, 16], P(('front', 'row', 'col')), may hold values from 0 to 63
- ranks: int32 [8, 4], P('front', 'row'), may hold values from 128 to 256
Outputs:
- sampled: float32 [8, 2048, 256], P('front', ('row', 'col'))
- bases: float32 [8, 2048, 256], P('front', ('row', 'col'))
The draws below stay inside these ranges and needn't reach their ends.
Inputs may be any that keep to these rules, and one draw needn't show every extreme that they name: `parent_front`: among the 2 tiles of one device, at most 2 name the same parent front.
All inputs are finite; a program needn't handle non-finite values.
Results may differ from the reference program's by a relative error of at most 0.0003.
Values may be sent and summed in bfloat16 or wider, within the bound.
No kernel may reach another device: no remote copies, remote signals or barrier semaphores. Data moves between devices by JAX's collectives and lax.ppermute only.
A program may use at most 64 MiB of HBM per device.

```python
import math
import jax
import jax.numpy as jnp
import numpy as np
from jax import lax

F = 8192
S = 256
LEAF = 512
CW = 2048
TILE_DEV = 2
ROWS = 2048
ROW_TILES = 16
PARENTS = 8
CAP = 2
TILES = 512
N_ROW = 4
N_COL = 8


def touch_ends(result, stream_key, low, largest):
    longest = result.shape.index(max(result.shape))
    spots = []
    for shift in (0, 1):
        where = [jax.random.randint(jax.random.fold_in(stream_key, axis), (), 0, length) for axis, length in enumerate(result.shape)]
        where[longest] = (where[longest] + shift) % result.shape[longest]
        spots.append(tuple(where))
    return result.at[spots[0]].set(low).at[spots[1]].set(largest)


def shard_levels(rng, extent, cuts, smallest, largest):
    factor_of, own = 1.0, jax.random.fold_in(rng, 6)
    for axis_at, parts in cuts:
        heights = jnp.exp(jax.random.uniform(jax.random.fold_in(own, axis_at), (parts,), jnp.float32, smallest / len(cuts), largest / len(cuts)))
        factor_of = factor_of * jnp.repeat(heights, extent[axis_at] // parts).reshape([-1 if axis == axis_at else 1 for axis in range(len(extent))])
    return factor_of


def routed_block(stream_key, own, number, rows, amount, top, reach, lean):
    ranking = jax.random.permutation(stream_key, amount)
    packed, ordinary = portions_of(amount, rows * top, reach, lean, True), portions_of(amount, rows * top, reach, lean, False)
    places = jnp.arange(amount)

    def named(sizes, offset_by):
        used = int((sizes > 0).sum())
        fixed = max(1, used // 4)
        shifted = fixed + (places - fixed + offset_by * (used - fixed)) % max(1, amount - fixed)
        return jnp.zeros((amount,), jnp.int32).at[ranking[jnp.where(places < fixed, places, shifted)]].set(jnp.asarray(sizes, jnp.int32))

    sizes = jnp.where(number % 4 == 0, named(packed, number // 4), named(ordinary, number - number // 4 - 1))
    mixed = jax.random.permutation(jax.random.fold_in(own, 3), amount)
    source_of, taker = mixed[0:amount // 2 * 2:2], mixed[1:amount // 2 * 2:2]
    margin = jnp.minimum(sizes[source_of] - 1, reach - sizes[taker]) // 2
    margin = jnp.where((source_of == ranking[0]) | (taker == ranking[0]) | (sizes[taker] == 0), 0, jnp.maximum(margin, 0))
    shifted = jax.random.randint(jax.random.fold_in(own, 4), (amount // 2,), 0, 1 << 20) % (margin + 1)
    sizes = sizes.at[source_of].add(-shifted).at[taker].add(shifted)
    items = jnp.searchsorted(jnp.cumsum(sizes), jnp.arange(rows * top), side="right").astype(jnp.int32)
    grid = items.reshape(top, rows).T
    grid = grid[jax.random.permutation(jax.random.fold_in(own, 1), rows)]
    offset_by = jax.random.randint(jax.random.fold_in(own, 2), (rows, 1), 0, top)
    return jnp.take_along_axis(grid, (jnp.arange(top)[None, :] + offset_by) % top, axis=1)


def portions_of(count, total, most, lean, full):
    loads = [(1 << 20) // math.isqrt(standing ** lean) + 1 for standing in range(1, count + 1)]
    largest = most if full else min(most, max(-(-total // count), total * loads[0] // sum(loads)))
    least = 1 if total - largest >= count - 1 else 0
    holding, surplus = [largest] + [least] * (count - 1), total - largest - least * (count - 1)
    while surplus > 0:
        candidates = [i for i in range(1, count) if holding[i] < largest] or [i for i in range(1, count) if holding[i] < most]
        whole, budget = sum([loads[i] for i in candidates]), surplus
        for i in candidates:
            addition = min(most - holding[i], max(1, budget * loads[i] // whole), surplus)
            holding[i] = holding[i] + addition
            surplus = surplus - addition
    return np.array(holding)


def normal_values(key, extent, scale, most, cuts=(), kind=jnp.bfloat16):
    array = jax.random.normal(key, extent, jnp.float32) * scale
    if len(cuts) > 0:
        array = shard_levels(key, extent, cuts, -0.22, 0.18) * array
    return jnp.clip(array, min=-most, max=most).astype(kind)


def setup_inputs(seed: int = 0) -> dict:
    key_list = jax.random.split(jax.random.key(seed), 8)
    front_slab = normal_values(key_list[0], (PARENTS, ROWS, F), F ** -0.5, 0.0625, ((0, 8), (1, 4), (2, 8)))
    samples = normal_values(key_list[1], (F, S), 1.0, 6.0, ((0, 32),))
    child_tiles = normal_values(key_list[2], (TILES, 128, CW), (CW * TILE_DEV * N_ROW * N_COL // ROW_TILES) ** -0.5, 0.0625, ((0, 256),))
    parent_front_keys = jax.random.split(jax.random.fold_in(key_list[3], 1), TILES // TILE_DEV)
    parent_front_turns = jax.random.permutation(jax.random.fold_in(key_list[3], 3), TILES // TILE_DEV)
    parent_front = jax.vmap(lambda own, number: routed_block(jax.random.fold_in(key_list[3], 2), own, number, TILE_DEV, PARENTS, 1, CAP, 2))(parent_front_keys, parent_front_turns).reshape((TILES, 1))
    parent_tile = touch_ends(jax.random.randint(key_list[4], (TILES,), 0, ROW_TILES), jax.random.fold_in(key_list[4], 1), 0, ROW_TILES - 1).astype(jnp.int32)
    column_tiles = touch_ends(jax.random.randint(key_list[5], (TILES, CW // 128), 0, F // 128), jax.random.fold_in(key_list[5], 1), 0, (F // 128) - 1).astype(jnp.int32)
    ranks = touch_ends(jax.random.randint(key_list[6], (PARENTS, N_ROW), S // 2, S + 1), jax.random.fold_in(key_list[6], 1), S // 2, S).astype(jnp.int32)
    return dict(front_slab=front_slab, samples=samples, child_tiles=child_tiles, parent_front=parent_front, parent_tile=parent_tile, column_tiles=column_tiles, ranks=ranks)


def leaf_basis(block, rank):
    width = block.shape[1]
    mask = (jnp.arange(width, dtype=jnp.int32) < rank).astype(jnp.float32)
    masked = block * mask[None, :]
    gram = jnp.dot(masked.T, masked, precision=lax.Precision.HIGHEST)
    gram = gram + jnp.diag(1.0 - mask)
    lower = jnp.linalg.cholesky(gram)
    return lax.linalg.triangular_solve(lower, masked, left_side=False, lower=True, transpose_a=True)

def reference(front_slab, samples, child_tiles, parent_front, parent_tile, column_tiles, ranks):
    parents = front_slab.shape[0]
    rows = front_slab.shape[1]
    full = front_slab.shape[2]
    width = samples.shape[1]
    tile_cols = child_tiles.shape[2]
    blocks = tile_cols // 128
    row_tiles = rows // 128
    omega_tiles = samples.reshape(full // 128, 128, width)
    devices = child_tiles.shape[0] // TILE_DEV
    tiles_blk = child_tiles.reshape(devices, TILE_DEV, 128, blocks, 128)
    dest_blk = parent_front.reshape(devices, TILE_DEV)
    place_blk = parent_tile.reshape(devices, TILE_DEV)
    cols_blk = column_tiles.reshape(devices, TILE_DEV, blocks)

    def step(acc, item):
        pieces, dest, place, cols = item
        chosen = omega_tiles[cols].astype(jnp.float32)
        product = jnp.einsum('trkc,tkcs->trs', pieces.astype(jnp.float32), chosen)
        key = (dest * row_tiles + place).astype(jnp.int32)
        return (acc.at[key].add(product), None)
    start = jnp.zeros((parents * row_tiles, 128, width), jnp.float32)
    extended, _ = lax.scan(step, start, (tiles_blk, dest_blk, place_blk, cols_blk))
    direct = lax.map(lambda slab: jnp.dot(slab.astype(jnp.float32), samples.astype(jnp.float32), preferred_element_type=jnp.float32), front_slab)
    sampled = direct + extended.reshape(parents, rows, width)
    leaves = sampled.reshape(parents * N_ROW, LEAF, width)
    bases = jax.vmap(leaf_basis)(leaves, ranks.reshape(-1))
    return (sampled, bases.reshape(parents, rows, width))
```

```python
import jax
import jax.numpy as jnp
import numpy as np
from jax import lax
from jax.experimental import pallas as pl
from jax.experimental.pallas import tpu as pltpu
from jax.sharding import Mesh, PartitionSpec as P

F32 = jnp.float32
PLANE = ("xh", "xl", "y")
VMEM = pl.BlockSpec(memory_space=pltpu.VMEM)
SMEM = pl.BlockSpec(memory_space=pltpu.SMEM)
PARAMS = pltpu.CompilerParams(vmem_limit_bytes=48 * 1024 * 1024)
LANES = 128


def sent_to_all(x, axis, count):
    copies = jnp.broadcast_to(x[None], (count, *x.shape))
    return lax.all_to_all(copies, axis, split_axis=0, concat_axis=0, tiled=True)


def products_kernel(meta, om, child0, child1, slab0, slab1, packed, direct):
    tails = []
    for t in range(4):
        child = (child0, child1)[t // 2]
        acc = jnp.zeros((128, LANES), F32)
        for b in range(0, 16, 2):
            one = om[pl.ds(pl.multiple_of(meta[16 * t + b] * 128, 128), 128), :]
            two = om[pl.ds(pl.multiple_of(meta[16 * t + b + 1] * 128, 128), 128), :]
            acc += jnp.dot(
                child[t % 2, :, 128 * b : 128 * b + 256],
                jnp.concatenate([one, two], axis=0),
                preferred_element_type=F32,
            )
        top = jnp.maximum(jnp.max(jnp.abs(acc), axis=0, keepdims=True), 1e-30)
        power = jnp.floor(jnp.log2(top)) + 1.0
        coded = jnp.round(acc * jnp.exp2(15.0 - power))
        coded = jnp.clip(coded, -32767.0, 32767.0)
        packed[128 * t : 128 * t + 128, :] = coded.astype(jnp.int32).astype(jnp.int16)
        tails.append(power.astype(jnp.int32))
    lane = lax.broadcasted_iota(jnp.int32, (1, LANES), 1)
    label = jnp.zeros((1, LANES), jnp.int32)
    for n in range(8):
        label = jnp.where(lane == n, meta[64 + n], label)
    rows = lax.broadcasted_iota(jnp.int32, (16, LANES), 0)
    tail = jnp.zeros((16, LANES), jnp.int32)
    for n, row in enumerate(tails + [label]):
        tail = jnp.where(rows == n, row, tail)
    packed[512:528, :] = tail.astype(jnp.int16)
    for o, slab in enumerate((slab0, slab1)):
        acc = jnp.zeros((512, LANES), F32)
        for b in range(4):
            start = pl.multiple_of(meta[72] + 512 * b, 256)
            acc += jnp.dot(
                slab[:, 256 * b : 256 * b + 256],
                om[pl.ds(start, 256), :],
                preferred_element_type=F32,
            )
        direct[o] = acc


def combine_kernel(meta, labels, arrived, direct, out):
    front, core, xh = meta[0], meta[1], meta[2]
    out[...] = jnp.zeros(out.shape, F32)
    for o in range(2):
        half = core if o == 0 else 1 - core
        start = pl.multiple_of(half * 64, 64)
        for c in range(8):
            out[xh * 8 + c, pl.ds(start, 64), :] = direct[o, 64 * c : 64 * c + 64, :]
    for s in range(8):
        for t in range(4):

            @pl.when(labels[s, t] == front)
            def _():
                j = labels[s, 4 + t]
                power = arrived[s, 512:528, :].astype(jnp.int32).astype(F32)[t : t + 1, :]
                tile = arrived[s, 128 * t : 128 * t + 128, :].astype(jnp.int32).astype(F32)
                tile = tile * jnp.exp2(power - 15.0)
                dest = (j // 8) * 8 + 2 * (j % 4)
                start = pl.multiple_of(((j // 4) % 2) * 64, 64)
                for h in range(2):
                    out[dest + h, pl.ds(start, 64), :] += tile[64 * h : 64 * h + 64, :]


def bases_kernel(meta, leaf, sampled, bases, aug):
    rank, at = meta[0], meta[1]
    n = 256
    keep = lax.broadcasted_iota(jnp.int32, (1, n), 1) < rank
    own = jnp.concatenate([leaf[0, at], leaf[1, at]], axis=1)
    sampled[...] = own
    full = jnp.concatenate([leaf[0].reshape(512, LANES), leaf[1].reshape(512, LANES)], axis=1)
    masked = jnp.where(keep, full, 0.0)
    gram = lax.dot_general(
        masked, masked, (((0,), (0,)), ((), ())),
        precision=lax.Precision.HIGHEST, preferred_element_type=F32,
    )
    r = lax.broadcasted_iota(jnp.int32, (n, n), 0)
    c = lax.broadcasted_iota(jnp.int32, (n, n), 1)
    aug[:, :n] = gram + jnp.where((r == c) & (c >= rank), 1.0, 0.0)
    mine = jnp.where(keep, own, 0.0)
    aug[:, n:] = jnp.concatenate([mine.T, jnp.zeros((n, 64), F32)], axis=1)
    width = 32
    row = lax.broadcasted_iota(jnp.int32, (width, 1), 0)
    for p in range(n // width):
        base = p * width
        panel = aug[base : base + width, :]
        done = []
        for j in range(width):
            pivot_row = panel[j : j + 1, :]
            column = panel[:, base + j : base + j + 1]
            pivot = column[j : j + 1, :]
            done.append(pivot_row * lax.rsqrt(pivot))
            factor = jnp.where(row > j, column * (1.0 / pivot), 0.0)
            panel = panel - factor * pivot_row
        panel = jnp.concatenate(done, axis=0)
        aug[base : base + width, :] = panel
        if base + width < n:
            rest = base + width
            update = lax.dot_general(
                panel[:, :n], panel, (((0,), (0,)), ((), ())),
                precision=lax.Precision.HIGHEST, preferred_element_type=F32,
            )
            aug[rest:, :] = aug[rest:, :] - update[rest:, :]
    bases[...] = aug[:, n : n + 64].T


def on_device(front_slab, samples, child_tiles, parent_front, parent_tile, column_tiles, ranks):
    front = lax.axis_index("z")
    core = lax.axis_index("core")
    xh = lax.axis_index("xh")
    col = lax.axis_index("xl") * 4 + lax.axis_index("y")
    swap = lambda x: lax.ppermute(x, "core", [(0, 1), (1, 0)])
    left, right = samples[:, :LANES], samples[:, LANES:]
    mine = jnp.where(core == 0, left, right)
    theirs = swap(jnp.where(core == 0, right, left))
    block = jnp.where(core == 0, jnp.stack([mine, theirs]), jnp.stack([theirs, mine]))
    omega = sent_to_all(block, PLANE, 16).reshape(-1, LANES)
    child0, slab0 = child_tiles, front_slab[0]
    child1, slab1 = swap(child0), swap(slab0)
    small = jnp.concatenate(
        [column_tiles.reshape(-1), parent_front[:, 0], parent_tile]
    )
    other = swap(small)
    tiles = jnp.concatenate([small[:32], other[:32]])
    block_of, half = tiles // 2, tiles % 2
    order = ((block_of // 16) * 8 + block_of % 8) * 2 + (block_of // 8) % 2
    first = (((col // 4) * 8 + (col % 2) * 4) * 2 + (col // 2) % 2) * 256
    meta = jnp.concatenate(
        [order * 2 + half, small[32:34], other[32:34], small[34:], other[34:], first[None]]
    ).astype(jnp.int32)
    packed, direct = pl.pallas_call(
        products_kernel,
        out_shape=(
            jax.ShapeDtypeStruct((528, LANES), jnp.int16),
            jax.ShapeDtypeStruct((2, 512, LANES), F32),
        ),
        in_specs=[SMEM] + [VMEM] * 5,
        out_specs=(VMEM, VMEM),
        compiler_params=PARAMS,
    )(meta, omega, child0, child1, slab0, slab1)
    arrived = sent_to_all(packed, "z", 8)
    labels = arrived[:, 516, :8].astype(jnp.int32)
    spread = pl.pallas_call(
        combine_kernel,
        out_shape=jax.ShapeDtypeStruct((16, 128, LANES), F32),
        in_specs=[SMEM, SMEM, VMEM, VMEM],
        out_specs=VMEM,
        compiler_params=PARAMS,
    )(jnp.stack([front, core, xh]).astype(jnp.int32), labels, arrived, direct)
    pieces = lax.all_to_all(spread, PLANE, 0, 0, tiled=True)
    rows = jnp.sum(pieces, axis=0).reshape(2, 1, 64, LANES)
    copies = jnp.broadcast_to(rows, (2, 8, 64, LANES)).reshape(16, 64, LANES)
    leaf = lax.all_to_all(copies, ("core", "xl", "y"), 0, 0, tiled=True)
    leaf = leaf.reshape(2, 8, 64, LANES)
    sampled, bases = pl.pallas_call(
        bases_kernel,
        out_shape=(
            jax.ShapeDtypeStruct((64, 256), F32),
            jax.ShapeDtypeStruct((64, 256), F32),
        ),
        in_specs=[SMEM, VMEM],
        out_specs=(VMEM, VMEM),
        scratch_shapes=[pltpu.VMEM((256, 384), F32)],
        compiler_params=PARAMS,
    )(jnp.stack([ranks[0, 0], col]).astype(jnp.int32), leaf)
    return sampled[None], bases[None]


def solution(mesh):
    split = Mesh(
        np.asarray(mesh.devices).reshape(8, 2, 2, 2, 4), ("z", "xh", "core", "xl", "y")
    )
    row, col = ("xh", "core"), ("xl", "y")
    in_specs = (
        P("z", row, col),
        P(row + col, None),
        P(("z",) + row + col, None, None),
        P(("z",) + row + col, None),
        P(("z",) + row + col),
        P(("z",) + row + col, None),
        P("z", row),
    )
    out_specs = (P("z", row + col, None), P("z", row + col, None))
    return jax.shard_map(
        on_device, mesh=split, in_specs=in_specs, out_specs=out_specs, check_vma=False
    )
```

```python
import jax
import jax.numpy as jnp
import numpy as np
from jax import lax
from jax.experimental import pallas as pl
from jax.experimental.pallas import tpu as pltpu
from jax.sharding import Mesh, PartitionSpec as P

F32 = jnp.float32
PLANE = ("xh", "xl", "y")
CORES = ("xh", "core", "xl", "y")
VMEM = pl.BlockSpec(memory_space=pltpu.VMEM)
SMEM = pl.BlockSpec(memory_space=pltpu.SMEM)
PARAMS = pltpu.CompilerParams(vmem_limit_bytes=48 * 1024 * 1024)
LANES = 128


def products_kernel(meta, omega, child0, child1, slab0, slab1, out):
    for t in range(4):
        child = (child0, child1)[t // 2]
        acc = jnp.zeros((128, LANES), F32)
        for b in range(0, 16, 2):
            one = omega[pl.ds(pl.multiple_of(meta[16 * t + b] * 128, 128), 128), :]
            two = omega[pl.ds(pl.multiple_of(meta[16 * t + b + 1] * 128, 128), 128), :]
            acc += jnp.dot(
                child[t % 2, :, 128 * b : 128 * b + 256],
                jnp.concatenate([one, two], axis=0),
                preferred_element_type=F32,
            )
        out[:, 8 * t : 8 * t + 8, :] = acc.reshape(16, 8, LANES)
    own = omega[pl.ds(pl.multiple_of(meta[72] * 1024, 1024), 1024), :]
    core = meta[73]
    for o, slab in enumerate((slab0, slab1)):
        half = core if o == 0 else 1 - core
        acc = jnp.dot(slab[...], own, preferred_element_type=F32).reshape(4, 16, 8, LANES)
        for q in range(4):
            start = pl.multiple_of(32 + half * 32 + 8 * q, 8)
            out[:, pl.ds(start, 8), :] = acc[q]
    lane = lax.broadcasted_iota(jnp.int32, (8, LANES), 1)
    label = jnp.zeros((8, LANES), jnp.int32)
    for n in range(8):
        label = jnp.where(lane == n, meta[64 + n], label)
    out[:, 96:104, :] = jnp.broadcast_to(label.astype(F32)[None], (16, 8, LANES))


def combine_kernel(labels, arrived, extended, direct):
    extended[...] = jnp.zeros(extended.shape, F32)
    for s in range(16):
        for t in range(4):
            start = pl.multiple_of(labels[s, 4 + t] * 8, 8)
            extended[labels[s, t], pl.ds(start, 8), :] += arrived[s, 8 * t : 8 * t + 8, :]
    for xh in range(2):
        total = arrived[8 * xh, 32:96, :]
        for c in range(1, 8):
            total += arrived[8 * xh + c, 32:96, :]
        direct[64 * xh : 64 * xh + 64, :] = total


def exact_dot(a, b):
    return lax.dot_general(
        a, b, (((0,), (0,)), ((), ())),
        precision=lax.Precision.HIGHEST, preferred_element_type=F32,
    )


def eliminated(panel, at, width, group):
    done = []
    wide = panel.shape[1] // LANES
    for g in range(0, width, group):
        rows = panel.shape[0]
        row = lax.broadcasted_iota(jnp.int32, (rows, LANES), 0)
        columns = [
            jnp.broadcast_to(panel[:, at + g + t : at + g + t + 1], (rows, LANES))
            for t in range(group)
        ]
        for t in range(group):
            pivot_row = panel[t : t + 1, :]
            pivot = columns[t][t : t + 1, :]
            factor = jnp.where(row > t, columns[t] * (1.0 / pivot), 0.0)
            done.append(pivot_row * jnp.concatenate([lax.rsqrt(pivot)] * wide, axis=1))
            for u in range(t + 1, group):
                columns[u] = columns[u] - factor * columns[u][t : t + 1, :]
            panel = panel - jnp.concatenate([factor] * wide, axis=1) * pivot_row
        panel = panel[group:, :]
    return jnp.concatenate(done, axis=0)


def bases_kernel(meta, leaf, sampled, bases, aug):
    rank, at = meta[0], meta[1]
    n = 256
    keep = lax.broadcasted_iota(jnp.int32, (1, n), 1) < rank
    own = jnp.concatenate(
        [leaf[at % 2, k, :, at // 2].reshape(64, LANES) for k in range(2)], axis=1
    )
    sampled[...] = own
    full = jnp.concatenate([leaf[:, k].reshape(512, LANES) for k in range(2)], axis=1)
    masked = jnp.where(keep, full, 0.0)
    r = lax.broadcasted_iota(jnp.int32, (n, n), 0)
    c = lax.broadcasted_iota(jnp.int32, (n, n), 1)
    aug[:, :n] = exact_dot(masked, masked) + jnp.where((r == c) & (c >= rank), 1.0, 0.0)
    mine = jnp.where(keep, own, 0.0)
    aug[:, n:] = jnp.concatenate([mine.T, jnp.zeros((n, 64), F32)], axis=1)
    width = 64
    for base in range(0, n, width):
        cut = base // LANES * LANES
        rest = base + width
        panel = eliminated(aug[base:rest, cut:], base - cut, width, 16)
        aug[base:rest, cut:] = panel
        if rest < n:
            low = rest // LANES * LANES
            tail = panel[:, low - cut :]
            update = exact_dot(tail[:, : n - low], tail)
            aug[rest:, low:] = aug[rest:, low:] - update[rest - low :, :]
    bases[...] = aug[:, n : n + 64].T


def on_device(front_slab, samples, child_tiles, parent_front, parent_tile, column_tiles, ranks):
    core = lax.axis_index("core")
    col = lax.axis_index("xl") * 4 + lax.axis_index("y")
    swap = lambda x: lax.ppermute(x, "core", [(0, 1), (1, 0)])
    halves = jnp.stack([samples[:, :LANES], samples[:, LANES:]])
    copies = jnp.broadcast_to(halves[None, :, None], (2, 2, 8, 256, LANES))
    omega = lax.all_to_all(copies.reshape(32, 256, LANES), CORES, 0, 0, tiled=True)
    child0, slab0 = child_tiles, front_slab[0]
    child1, slab1 = swap(child0), swap(slab0)
    small = jnp.concatenate([column_tiles.reshape(-1), parent_front[:, 0], parent_tile])
    other = swap(small)
    meta = jnp.concatenate(
        [small[:32], other[:32], small[32:34], other[32:34], small[34:], other[34:]]
        + [jnp.stack([col, core]).astype(jnp.int32)]
    )
    out = pl.pallas_call(
        products_kernel,
        out_shape=jax.ShapeDtypeStruct((16, 104, LANES), F32),
        in_specs=[SMEM] + [VMEM] * 5,
        out_specs=VMEM,
        compiler_params=PARAMS,
    )(meta, omega.reshape(-1, LANES), child0, child1, slab0, slab1)
    arrived = lax.all_to_all(out, PLANE, 0, 0, tiled=True)
    labels = arrived[:, 96, :8].astype(jnp.int32)
    extended, direct = pl.pallas_call(
        combine_kernel,
        out_shape=(
            jax.ShapeDtypeStruct((8, 128, LANES), F32),
            jax.ShapeDtypeStruct((128, LANES), F32),
        ),
        in_specs=[SMEM, VMEM],
        out_specs=(VMEM, VMEM),
        compiler_params=PARAMS,
    )(labels, arrived)
    pieces = lax.all_to_all(extended, "z", 0, 0, tiled=True)
    rows = (direct + jnp.sum(pieces, axis=0)).reshape(4, 1, 32, LANES)
    copies = jnp.broadcast_to(rows, (4, 8, 32, LANES)).reshape(32, 32, LANES)
    leaf = lax.all_to_all(copies, CORES, 0, 0, tiled=True)
    sampled, bases = pl.pallas_call(
        bases_kernel,
        out_shape=(
            jax.ShapeDtypeStruct((64, 256), F32),
            jax.ShapeDtypeStruct((64, 256), F32),
        ),
        in_specs=[SMEM, VMEM],
        out_specs=(VMEM, VMEM),
        scratch_shapes=[pltpu.VMEM((256, 384), F32)],
        compiler_params=PARAMS,
    )(jnp.stack([ranks[0, 0], col]).astype(jnp.int32), leaf.reshape(2, 2, 8, 4, 8, LANES))
    return sampled[None], bases[None]


def solution(mesh):
    split = Mesh(
        np.asarray(mesh.devices).reshape(8, 2, 2, 2, 4), ("z", "xh", "core", "xl", "y")
    )
    row, col = ("xh", "core"), ("xl", "y")
    in_specs = (
        P("z", row, col),
        P(row + col, None),
        P(("z",) + row + col, None, None),
        P(("z",) + row + col, None),
        P(("z",) + row + col),
        P(("z",) + row + col, None),
        P("z", row),
    )
    out_specs = (P("z", row + col, None), P("z", row + col, None))
    return jax.shard_map(
        on_device, mesh=split, in_specs=in_specs, out_specs=out_specs, check_vma=False
    )
```

```python
import jax
import jax.numpy as jnp
import numpy as np
from jax import lax
from jax.experimental import pallas as pl
from jax.experimental.pallas import tpu as pltpu
from jax.sharding import Mesh, PartitionSpec as P

F32 = jnp.float32
PLANE = ("xh", "xl", "y")
CORES = ("xh", "core", "xl", "y")
VMEM = pl.BlockSpec(memory_space=pltpu.VMEM)
SMEM = pl.BlockSpec(memory_space=pltpu.SMEM)
PARAMS = pltpu.CompilerParams(vmem_limit_bytes=48 * 1024 * 1024)
LANES = 128


def products_kernel(
    meta, part0, part1, part2, part3, child0_in, child1_in, slab0_in, slab1_in, out,
    omega, child0, child1, slab0, slab1, sems,
):
    copies = [
        pltpu.make_async_copy(source, target, sems.at[n])
        for n, (source, target) in enumerate(
            [
                (child0_in, child0),
                (part0, omega.at[pl.ds(0, 2048)]),
                (part1, omega.at[pl.ds(2048, 2048)]),
                (part2, omega.at[pl.ds(4096, 2048)]),
                (part3, omega.at[pl.ds(6144, 2048)]),
                (child1_in, child1),
                (slab0_in, slab0),
                (slab1_in, slab1),
            ]
        )
    ]
    for copy in copies:
        copy.start()
    lane = lax.broadcasted_iota(jnp.int32, (8, LANES), 1)
    label = jnp.zeros((8, LANES), jnp.int32)
    for n in range(8):
        label = jnp.where(lane == n, meta[64 + n], label)
    out[:, 96:104, :] = jnp.broadcast_to(label.astype(F32)[None], (16, 8, LANES))
    for n in range(5):
        copies[n].wait()
    for t in range(4):
        if t == 2:
            copies[5].wait()
        child = (child0, child1)[t // 2]
        acc = jnp.zeros((128, LANES), F32)
        for b in range(0, 16, 2):
            one = omega[pl.ds(pl.multiple_of(meta[16 * t + b] * 128, 128), 128), :]
            two = omega[pl.ds(pl.multiple_of(meta[16 * t + b + 1] * 128, 128), 128), :]
            acc += jnp.dot(
                child[t % 2, :, 128 * b : 128 * b + 256],
                jnp.concatenate([one, two], axis=0),
                preferred_element_type=F32,
            )
        out[:, 8 * t : 8 * t + 8, :] = acc.reshape(16, 8, LANES)
    own = jnp.concatenate(
        [omega[pl.ds(pl.multiple_of(meta[72 + b] * 256, 256), 256), :] for b in range(4)], axis=0
    )
    core = meta[76]
    for o, slab in enumerate((slab0, slab1)):
        copies[6 + o].wait()
        half = core if o == 0 else 1 - core
        acc = jnp.dot(slab[...], own, preferred_element_type=F32).reshape(4, 16, 8, LANES)
        for q in range(4):
            start = pl.multiple_of(32 + half * 32 + 8 * q, 8)
            out[:, pl.ds(start, 8), :] = acc[q]


def combine_kernel(labels, arrived, extended, direct):
    extended[...] = jnp.zeros(extended.shape, F32)
    for s in range(16):
        for t in range(4):
            start = pl.multiple_of(labels[s, 4 + t] * 8, 8)
            extended[labels[s, t], pl.ds(start, 8), :] += arrived[s, 8 * t : 8 * t + 8, :]
    for xh in range(2):
        total = arrived[8 * xh, 32:96, :]
        for c in range(1, 8):
            total += arrived[8 * xh + c, 32:96, :]
        direct[64 * xh : 64 * xh + 64, :] = total


def exact_dot(a, b):
    return lax.dot_general(
        a, b, (((0,), (0,)), ((), ())),
        precision=lax.Precision.HIGHEST, preferred_element_type=F32,
    )


def eliminated(panel, at, width, group):
    done = []
    wide = panel.shape[1] // LANES
    for g in range(0, width, group):
        rows = panel.shape[0]
        row = lax.broadcasted_iota(jnp.int32, (rows, LANES), 0)
        columns = [
            jnp.broadcast_to(panel[:, at + g + t : at + g + t + 1], (rows, LANES))
            for t in range(group)
        ]
        for t in range(group):
            pivot_row = panel[t : t + 1, :]
            pivot = columns[t][t : t + 1, :]
            factor = jnp.where(row > t, columns[t] * (1.0 / pivot), 0.0)
            done.append(pivot_row * jnp.concatenate([lax.rsqrt(pivot)] * wide, axis=1))
            for u in range(t + 1, group):
                columns[u] = columns[u] - factor * columns[u][t : t + 1, :]
            panel = panel - jnp.concatenate([factor] * wide, axis=1) * pivot_row
        panel = panel[group:, :]
    return jnp.concatenate(done, axis=0)


def bases_kernel(meta, leaf, sampled, bases, aug):
    rank, at = meta[0], meta[1]
    n = 256
    keep = lax.broadcasted_iota(jnp.int32, (1, n), 1) < rank
    own = jnp.concatenate(
        [leaf[at % 2, k, :, at // 2].reshape(64, LANES) for k in range(2)], axis=1
    )
    sampled[...] = own
    full = jnp.concatenate([leaf[:, k].reshape(512, LANES) for k in range(2)], axis=1)
    masked = jnp.where(keep, full, 0.0)
    r = lax.broadcasted_iota(jnp.int32, (n, n), 0)
    c = lax.broadcasted_iota(jnp.int32, (n, n), 1)
    aug[:, :n] = exact_dot(masked, masked) + jnp.where((r == c) & (c >= rank), 1.0, 0.0)
    mine = jnp.where(keep, own, 0.0)
    aug[:, n:] = jnp.concatenate([mine.T, jnp.zeros((n, 64), F32)], axis=1)
    width = 64
    for base in range(0, n, width):
        cut = base // LANES * LANES
        rest = base + width
        panel = eliminated(aug[base:rest, cut:], base - cut, width, 16)
        aug[base:rest, cut:] = panel
        if rest < n:
            low = rest // LANES * LANES
            tail = panel[:, low - cut :]
            update = exact_dot(tail[:, : n - low], tail)
            aug[rest:, low:] = aug[rest:, low:] - update[rest - low :, :]
    bases[...] = aug[:, n : n + 64].T


def ringed(v, stage, shift):
    pairs = []
    for n in range(32):
        xh, core, xl, y = n // 16, n // 8 % 2, n // 4 % 2, n % 4
        x = xh * 2 + xl
        if core == stage:
            y = (y + shift) % 4
        else:
            x = (x + shift) % 4
        pairs.append((n, ((x // 2 * 2 + core) * 2 + x % 2) * 4 + y))
    return lax.ppermute(v, CORES, pairs)


def on_device(front_slab, samples, child_tiles, parent_front, parent_tile, column_tiles, ranks):
    core, xh, xl, y = (lax.axis_index(name) for name in ("core", "xh", "xl", "y"))
    col, x = xl * 4 + y, xh * 2 + xl
    swap = lambda v: lax.ppermute(v, "core", [(0, 1), (1, 0)])
    left, right = samples[:, :LANES], samples[:, LANES:]
    mine = jnp.where(core == 0, left, right)
    block = jnp.concatenate([mine, swap(jnp.where(core == 0, right, left))], axis=0)
    line = jnp.concatenate([block] + [ringed(block, 0, k) for k in (1, 2, 3)], axis=0)
    parts = [line] + [ringed(line, 1, k) for k in (1, 2, 3)]
    child0, slab0 = child_tiles, front_slab[0]
    child1, slab1 = swap(child0), swap(slab0)
    small = jnp.concatenate([column_tiles.reshape(-1), parent_front[:, 0], parent_tile])
    other = swap(small)
    mine_first = (col // 2) * 8 + (col % 2) * 4 + jnp.arange(4)
    blocks = jnp.concatenate([small[:32] // 2, other[:32] // 2, mine_first])
    dx = (x - (blocks // 16) * 2 - (blocks // 4) % 2) % 4
    dy = (y - blocks) % 4
    place = jnp.where(core == 0, dx * 4 + dy, dy * 4 + dx) * 2 + (blocks // 8 + core) % 2
    odd = jnp.concatenate([small[:32], other[:32]]) % 2
    meta = jnp.concatenate(
        [place[:64] * 2 + odd, small[32:34], other[32:34], small[34:], other[34:]]
        + [place[64:], core[None]]
    ).astype(jnp.int32)
    ANY = pl.BlockSpec(memory_space=pl.ANY)
    out = pl.pallas_call(
        products_kernel,
        out_shape=jax.ShapeDtypeStruct((16, 104, LANES), F32),
        in_specs=[SMEM] + [ANY] * 8,
        out_specs=VMEM,
        scratch_shapes=[
            pltpu.VMEM((8192, LANES), jnp.bfloat16),
            pltpu.VMEM((2, 128, 2048), jnp.bfloat16),
            pltpu.VMEM((2, 128, 2048), jnp.bfloat16),
            pltpu.VMEM((512, 1024), jnp.bfloat16),
            pltpu.VMEM((512, 1024), jnp.bfloat16),
            pltpu.SemaphoreType.DMA((8,)),
        ],
        compiler_params=PARAMS,
    )(meta, *parts, child0, child1, slab0, slab1)
    arrived = lax.all_to_all(out, PLANE, 0, 0, tiled=True)
    labels = arrived[:, 96, :8].astype(jnp.int32)
    extended, direct = pl.pallas_call(
        combine_kernel,
        out_shape=(
            jax.ShapeDtypeStruct((8, 128, LANES), F32),
            jax.ShapeDtypeStruct((128, LANES), F32),
        ),
        in_specs=[SMEM, VMEM],
        out_specs=(VMEM, VMEM),
        compiler_params=PARAMS,
    )(labels, arrived)
    pieces = lax.all_to_all(extended, "z", 0, 0, tiled=True)
    rows = (direct + jnp.sum(pieces, axis=0)).reshape(4, 1, 32, LANES)
    copies = jnp.broadcast_to(rows, (4, 8, 32, LANES)).reshape(32, 32, LANES)
    leaf = lax.all_to_all(copies, CORES, 0, 0, tiled=True)
    sampled, bases = pl.pallas_call(
        bases_kernel,
        out_shape=(
            jax.ShapeDtypeStruct((64, 256), F32),
            jax.ShapeDtypeStruct((64, 256), F32),
        ),
        in_specs=[SMEM, VMEM],
        out_specs=(VMEM, VMEM),
        scratch_shapes=[pltpu.VMEM((256, 384), F32)],
        compiler_params=PARAMS,
    )(jnp.stack([ranks[0, 0], col]).astype(jnp.int32), leaf.reshape(2, 2, 8, 4, 8, LANES))
    return sampled[None], bases[None]


def solution(mesh):
    split = Mesh(
        np.asarray(mesh.devices).reshape(8, 2, 2, 2, 4), ("z", "xh", "core", "xl", "y")
    )
    row, col = ("xh", "core"), ("xl", "y")
    in_specs = (
        P("z", row, col),
        P(row + col, None),
        P(("z",) + row + col, None, None),
        P(("z",) + row + col, None),
        P(("z",) + row + col),
        P(("z",) + row + col, None),
        P("z", row),
    )
    out_specs = (P("z", row + col, None), P("z", row + col, None))
    return jax.shard_map(
        on_device, mesh=split, in_specs=in_specs, out_specs=out_specs, check_vma=False
    )
```

```python
import jax
import jax.numpy as jnp
import numpy as np
from jax import lax
from jax.experimental import pallas as pl
from jax.experimental.pallas import tpu as pltpu
from jax.sharding import Mesh, PartitionSpec as P

F32 = jnp.float32
PLANE = ("xh", "xl", "y")
CORES = ("xh", "core", "xl", "y")
VMEM = pl.BlockSpec(memory_space=pltpu.VMEM)
SMEM = pl.BlockSpec(memory_space=pltpu.SMEM)
PARAMS = pltpu.CompilerParams(vmem_limit_bytes=16 * 1024 * 1024)
LANES = 128


def products_kernel(meta, omega, child0, child1, slab0, slab1, out):
    lane = lax.broadcasted_iota(jnp.int32, (8, LANES), 1)
    label = jnp.zeros((8, LANES), jnp.int32)
    for n in range(8):
        label = jnp.where(lane == n, meta[64 + n], label)
    out[:, 96:104, :] = jnp.broadcast_to(label.astype(F32)[None], (16, 8, LANES))
    for t in range(4):
        child = (child0, child1)[t // 2]
        acc = jnp.zeros((128, LANES), F32)
        for b in range(0, 16, 2):
            one = omega[pl.ds(pl.multiple_of(meta[16 * t + b] * 128, 128), 128), :]
            two = omega[pl.ds(pl.multiple_of(meta[16 * t + b + 1] * 128, 128), 128), :]
            acc += jnp.dot(
                child[t % 2, :, 128 * b : 128 * b + 256],
                jnp.concatenate([one, two], axis=0),
                preferred_element_type=F32,
            )
        out[:, 8 * t : 8 * t + 8, :] = acc.reshape(16, 8, LANES)
    own = jnp.concatenate(
        [omega[pl.ds(pl.multiple_of(meta[72 + b] * 256, 256), 256), :] for b in range(4)], axis=0
    )
    core = meta[76]
    for o, slab in enumerate((slab0, slab1)):
        half = core if o == 0 else 1 - core
        acc = jnp.dot(slab[...], own, preferred_element_type=F32).reshape(4, 16, 8, LANES)
        for q in range(4):
            start = pl.multiple_of(32 + half * 32 + 8 * q, 8)
            out[:, pl.ds(start, 8), :] = acc[q]


def combine_kernel(labels, arrived, extended, direct):
    extended[...] = jnp.zeros(extended.shape, F32)
    for s in range(16):
        for t in range(4):
            start = pl.multiple_of(labels[s, 4 + t] * 8, 8)
            extended[labels[s, t], pl.ds(start, 8), :] += arrived[s, 8 * t : 8 * t + 8, :]
    for xh in range(2):
        total = arrived[8 * xh, 32:96, :]
        for c in range(1, 8):
            total += arrived[8 * xh + c, 32:96, :]
        direct[64 * xh : 64 * xh + 64, :] = total


def spread_kernel(pieces, direct, out):
    for n in range(4):
        total = direct[32 * n : 32 * n + 32, :]
        for z in range(8):
            total += pieces[z, 32 * n : 32 * n + 32, :]
        for c in range(8):
            out[8 * n + c] = total


def exact_dot(a, b):
    return lax.dot_general(
        a, b, (((0,), (0,)), ((), ())),
        precision=lax.Precision.HIGHEST, preferred_element_type=F32,
    )


def eliminated(panel, at, width, group):
    done = []
    wide = panel.shape[1] // LANES
    for g in range(0, width, group):
        rows = panel.shape[0]
        row = lax.broadcasted_iota(jnp.int32, (rows, LANES), 0)
        columns = [
            jnp.broadcast_to(panel[:, at + g + t : at + g + t + 1], (rows, LANES))
            for t in range(group)
        ]
        for t in range(group):
            pivot_row = panel[t : t + 1, :]
            pivot = columns[t][t : t + 1, :]
            factor = jnp.where(row > t, columns[t] * (1.0 / pivot), 0.0)
            done.append(pivot_row * jnp.concatenate([lax.rsqrt(pivot)] * wide, axis=1))
            for u in range(t + 1, group):
                columns[u] = columns[u] - factor * columns[u][t : t + 1, :]
            panel = panel - jnp.concatenate([factor] * wide, axis=1) * pivot_row
        panel = panel[group:, :]
    return jnp.concatenate(done, axis=0)


def bases_kernel(meta, leaf, sampled, bases, aug):
    rank, at = meta[0], meta[1]
    n = 256
    keep = lax.broadcasted_iota(jnp.int32, (1, n), 1) < rank
    own = jnp.concatenate(
        [leaf[at % 2, k, :, at // 2].reshape(64, LANES) for k in range(2)], axis=1
    )
    sampled[...] = own
    full = jnp.concatenate([leaf[:, k].reshape(512, LANES) for k in range(2)], axis=1)
    masked = jnp.where(keep, full, 0.0)
    r = lax.broadcasted_iota(jnp.int32, (n, n), 0)
    c = lax.broadcasted_iota(jnp.int32, (n, n), 1)
    aug[:, :n] = exact_dot(masked, masked) + jnp.where((r == c) & (c >= rank), 1.0, 0.0)
    mine = jnp.where(keep, own, 0.0)
    aug[:, n:] = jnp.concatenate([mine.T, jnp.zeros((n, 64), F32)], axis=1)
    width = 64
    for base in range(0, n, width):
        cut = base // LANES * LANES
        rest = base + width
        panel = eliminated(aug[base:rest, cut:], base - cut, width, 16)
        aug[base:rest, cut:] = panel
        if rest < n:
            low = rest // LANES * LANES
            tail = panel[:, low - cut :]
            update = exact_dot(tail[:, : n - low], tail)
            aug[rest:, low:] = aug[rest:, low:] - update[rest - low :, :]
    bases[...] = aug[:, n : n + 64].T


def ringed(v, stage, shift):
    pairs = []
    for n in range(32):
        xh, core, xl, y = n // 16, n // 8 % 2, n // 4 % 2, n % 4
        x = xh * 2 + xl
        if core == stage:
            y = (y + shift) % 4
        else:
            x = (x + shift) % 4
        pairs.append((n, ((x // 2 * 2 + core) * 2 + x % 2) * 4 + y))
    return lax.ppermute(v, CORES, pairs)


def on_device(front_slab, samples, child_tiles, parent_front, parent_tile, column_tiles, ranks):
    core, xh, xl, y = (lax.axis_index(name) for name in ("core", "xh", "xl", "y"))
    col, x = xl * 4 + y, xh * 2 + xl
    swap = lambda v: lax.ppermute(v, "core", [(0, 1), (1, 0)])
    left, right = samples[:, :LANES], samples[:, LANES:]
    mine = jnp.where(core == 0, left, right)
    block = jnp.concatenate([mine, swap(jnp.where(core == 0, right, left))], axis=0)
    child0, slab0 = child_tiles, front_slab[0]
    child1, slab1 = swap(child0), swap(slab0)
    block, column_tiles, parent_front, parent_tile = lax.optimization_barrier(
        (block, column_tiles, parent_front, parent_tile)
    )
    line = jnp.concatenate([block] + [ringed(block, 0, k) for k in (1, 2, 3)], axis=0)
    parts = [line] + [ringed(line, 1, k) for k in (1, 2, 3)]
    small = jnp.concatenate([column_tiles.reshape(-1), parent_front[:, 0], parent_tile])
    other = swap(small)
    mine_first = (col // 2) * 8 + (col % 2) * 4 + jnp.arange(4)
    blocks = jnp.concatenate([small[:32] // 2, other[:32] // 2, mine_first])
    dx = (x - (blocks // 16) * 2 - (blocks // 4) % 2) % 4
    dy = (y - blocks) % 4
    place = jnp.where(core == 0, dx * 4 + dy, dy * 4 + dx) * 2 + (blocks // 8 + core) % 2
    odd = jnp.concatenate([small[:32], other[:32]]) % 2
    meta = jnp.concatenate(
        [place[:64] * 2 + odd, small[32:34], other[32:34], small[34:], other[34:]]
        + [place[64:], core[None]]
    ).astype(jnp.int32)
    out = pl.pallas_call(
        products_kernel,
        out_shape=jax.ShapeDtypeStruct((16, 104, LANES), F32),
        in_specs=[SMEM] + [VMEM] * 5,
        out_specs=VMEM,
        compiler_params=PARAMS,
    )(meta, jnp.concatenate(parts, axis=0), child0, child1, slab0, slab1)
    arrived = lax.all_to_all(out, PLANE, 0, 0, tiled=True)
    labels = arrived[:, 96, :8].astype(jnp.int32)
    turned = (core == 1) & (jnp.arange(8) < 4)
    labels = jnp.where(turned, 7 - labels, labels)
    extended, direct = pl.pallas_call(
        combine_kernel,
        out_shape=(
            jax.ShapeDtypeStruct((8, 128, LANES), F32),
            jax.ShapeDtypeStruct((128, LANES), F32),
        ),
        in_specs=[SMEM, VMEM],
        out_specs=(VMEM, VMEM),
        compiler_params=PARAMS,
    )(labels, arrived)
    groups = [
        [z * 32 + n for z in (range(8) if n // 8 % 2 == 0 else range(7, -1, -1))]
        for n in range(32)
    ]
    pieces = lax.all_to_all(
        extended, ("z",) + CORES, 0, 0, tiled=True, axis_index_groups=groups
    )
    copies = pl.pallas_call(
        spread_kernel,
        out_shape=jax.ShapeDtypeStruct((32, 32, LANES), F32),
        in_specs=[VMEM, VMEM],
        out_specs=VMEM,
        compiler_params=PARAMS,
    )(pieces, direct)
    leaf = lax.all_to_all(copies, CORES, 0, 0, tiled=True)
    sampled, bases = pl.pallas_call(
        bases_kernel,
        out_shape=(
            jax.ShapeDtypeStruct((64, 256), F32),
            jax.ShapeDtypeStruct((64, 256), F32),
        ),
        in_specs=[SMEM, VMEM],
        out_specs=(VMEM, VMEM),
        scratch_shapes=[pltpu.VMEM((256, 384), F32)],
        compiler_params=PARAMS,
    )(jnp.stack([ranks[0, 0], col]).astype(jnp.int32), leaf.reshape(2, 2, 8, 4, 8, LANES))
    return sampled[None], bases[None]


def solution(mesh):
    split = Mesh(
        np.asarray(mesh.devices).reshape(8, 2, 2, 2, 4), ("z", "xh", "core", "xl", "y")
    )
    row, col = ("xh", "core"), ("xl", "y")
    in_specs = (
        P("z", row, col),
        P(row + col, None),
        P(("z",) + row + col, None, None),
        P(("z",) + row + col, None),
        P(("z",) + row + col),
        P(("z",) + row + col, None),
        P("z", row),
    )
    out_specs = (P("z", row + col, None), P("z", row + col, None))
    return jax.shard_map(
        on_device, mesh=split, in_specs=in_specs, out_specs=out_specs, check_vma=False
    )
```

```python
import jax
import jax.numpy as jnp
import numpy as np
from jax import lax
from jax.experimental import pallas as pl
from jax.experimental.pallas import tpu as pltpu
from jax.sharding import Mesh, PartitionSpec as P

F32 = jnp.float32
PLANE = ("xh", "xl", "y")
CORES = ("xh", "core", "xl", "y")
VMEM = pl.BlockSpec(memory_space=pltpu.VMEM)
SMEM = pl.BlockSpec(memory_space=pltpu.SMEM)
PARAMS = pltpu.CompilerParams(vmem_limit_bytes=50 * 1024 * 1024)
LANES = 128


def products_kernel(meta, *refs):
    parts, inputs, out, omega, sems = refs[:8], refs[8:12], refs[12], refs[13], refs[18]
    child0, child1, slab0, slab1 = refs[14:18]
    copies = [
        pltpu.make_async_copy(part, omega.at[pl.ds(1024 * n, 1024)], sems.at[n])
        for n, part in enumerate(parts)
    ] + [
        pltpu.make_async_copy(source, target, sems.at[8 + n])
        for n, (source, target) in enumerate(zip(inputs, refs[14:18]))
    ]
    for copy in copies:
        copy.start()
    lane = lax.broadcasted_iota(jnp.int32, (8, LANES), 1)
    label = jnp.zeros((8, LANES), jnp.int32)
    for n in range(8):
        label = jnp.where(lane == n, meta[64 + n], label)
    out[:, 96:104, :] = jnp.broadcast_to(label.astype(F32)[None], (16, 8, LANES))
    for copy in copies[:9]:
        copy.wait()
    for t in range(4):
        if t == 2:
            copies[9].wait()
        child = (child0, child1)[t // 2]
        acc = jnp.zeros((128, LANES), F32)
        for b in range(0, 16, 2):
            one = omega[pl.ds(pl.multiple_of(meta[16 * t + b] * 128, 128), 128), :]
            two = omega[pl.ds(pl.multiple_of(meta[16 * t + b + 1] * 128, 128), 128), :]
            acc += jnp.dot(
                child[t % 2, :, 128 * b : 128 * b + 256],
                jnp.concatenate([one, two], axis=0),
                preferred_element_type=F32,
            )
        out[:, 8 * t : 8 * t + 8, :] = acc.reshape(16, 8, LANES)
    own = jnp.concatenate(
        [omega[pl.ds(pl.multiple_of(meta[72 + b] * 256, 256), 256), :] for b in range(4)], axis=0
    )
    core = meta[76]
    for o, slab in enumerate((slab0, slab1)):
        copies[10 + o].wait()
        half = core if o == 0 else 1 - core
        acc = jnp.dot(slab[...], own, preferred_element_type=F32).reshape(4, 16, 8, LANES)
        for q in range(4):
            start = pl.multiple_of(32 + half * 32 + 8 * q, 8)
            out[:, pl.ds(start, 8), :] = acc[q]


def combine_kernel(labels, arrived, coded, direct, extended):
    extended[...] = jnp.zeros(extended.shape, F32)
    for s in range(16):
        for t in range(4):
            start = pl.multiple_of(labels[s, 4 + t] * 8, 8)
            extended[labels[s, t], pl.ds(start, 8), :] += arrived[s, 8 * t : 8 * t + 8, :]
    for p in range(8):
        value = extended[p].reshape(16, 8, LANES)
        top = jnp.maximum(jnp.max(jnp.abs(value), axis=1), 1e-30)
        power = jnp.floor(jnp.log2(top)) + 1.0
        scaled = jnp.round(value * jnp.exp2(15.0 - power)[:, None, :])
        scaled = jnp.clip(scaled, -32767.0, 32767.0).reshape(128, LANES)
        coded[p, :128, :] = scaled.astype(jnp.int32).astype(jnp.int16)
        coded[p, 128:, :] = power.astype(jnp.int32).astype(jnp.int16)
    for xh in range(2):
        total = arrived[8 * xh, 32:96, :]
        for c in range(1, 8):
            total += arrived[8 * xh + c, 32:96, :]
        direct[64 * xh : 64 * xh + 64, :] = total


def spread_kernel(pieces, direct, out):
    total = direct[...].reshape(16, 8, LANES)
    for z in range(8):
        power = pieces[z, 128:, :].astype(jnp.int32).astype(F32)
        value = pieces[z, :128, :].astype(jnp.int32).astype(F32).reshape(16, 8, LANES)
        total += value * jnp.exp2(power - 15.0)[:, None, :]
    total = total.reshape(4, 32, LANES)
    for n in range(4):
        for c in range(8):
            out[8 * n + c] = total[n]


def exact_dot(a, b):
    return lax.dot_general(
        a, b, (((0,), (0,)), ((), ())),
        precision=lax.Precision.HIGHEST, preferred_element_type=F32,
    )


def eliminated(panel, at, width, group):
    done = []
    wide = panel.shape[1] // LANES
    for g in range(0, width, group):
        rows = panel.shape[0]
        row = lax.broadcasted_iota(jnp.int32, (rows, LANES), 0)
        columns = [
            jnp.broadcast_to(panel[:, at + g + t : at + g + t + 1], (rows, LANES))
            for t in range(group)
        ]
        for t in range(group):
            pivot_row = panel[t : t + 1, :]
            pivot = columns[t][t : t + 1, :]
            factor = jnp.where(row > t, columns[t] * (1.0 / pivot), 0.0)
            done.append(pivot_row * jnp.concatenate([lax.rsqrt(pivot)] * wide, axis=1))
            for u in range(t + 1, group):
                columns[u] = columns[u] - factor * columns[u][t : t + 1, :]
            panel = panel - jnp.concatenate([factor] * wide, axis=1) * pivot_row
        panel = panel[group:, :]
    return jnp.concatenate(done, axis=0)


def bases_kernel(meta, leaf, sampled, bases, aug):
    rank, at = meta[0], meta[1]
    n = 256
    keep = lax.broadcasted_iota(jnp.int32, (1, n), 1) < rank
    own = jnp.concatenate(
        [leaf[at % 2, k, :, at // 2].reshape(64, LANES) for k in range(2)], axis=1
    )
    sampled[...] = own
    full = jnp.concatenate([leaf[:, k].reshape(512, LANES) for k in range(2)], axis=1)
    masked = jnp.where(keep, full, 0.0)
    r = lax.broadcasted_iota(jnp.int32, (n, n), 0)
    c = lax.broadcasted_iota(jnp.int32, (n, n), 1)
    aug[:, :n] = exact_dot(masked, masked) + jnp.where((r == c) & (c >= rank), 1.0, 0.0)
    mine = jnp.where(keep, own, 0.0)
    aug[:, n:] = jnp.concatenate([mine.T, jnp.zeros((n, 64), F32)], axis=1)
    width = 64
    for base in range(0, n, width):
        cut = base // LANES * LANES
        rest = base + width
        panel = eliminated(aug[base:rest, cut:], base - cut, width, 16)
        aug[base:rest, cut:] = panel
        if rest < n:
            low = rest // LANES * LANES
            tail = panel[:, low - cut :]
            update = exact_dot(tail[:, : n - low], tail)
            aug[rest:, low:] = aug[rest:, low:] - update[rest - low :, :]
    bases[...] = aug[:, n : n + 64].T


def ringed(v, stage, shift):
    pairs = []
    for n in range(32):
        xh, core, xl, y = n // 16, n // 8 % 2, n // 4 % 2, n % 4
        x = xh * 2 + xl
        if core == stage:
            y = (y + shift) % 4
        else:
            x = (x + shift) % 4
        pairs.append((n, ((x // 2 * 2 + core) * 2 + x % 2) * 4 + y))
    return lax.ppermute(v, CORES, pairs)


def on_device(front_slab, samples, child_tiles, parent_front, parent_tile, column_tiles, ranks):
    core, xh, xl, y = (lax.axis_index(name) for name in ("core", "xh", "xl", "y"))
    col, x = xl * 4 + y, xh * 2 + xl
    swap = lambda v: lax.ppermute(v, "core", [(0, 1), (1, 0)])
    left, right = samples[:, :LANES], samples[:, LANES:]
    mine = jnp.where(core == 0, left, right)
    block = jnp.concatenate([mine, swap(jnp.where(core == 0, right, left))], axis=0)
    child0, slab0 = child_tiles, front_slab[0]
    child1, slab1 = swap(child0), swap(slab0)
    near = ringed(block, 0, 1)
    line = [jnp.concatenate([block, near], axis=0)]
    line.append(jnp.concatenate([ringed(block, 0, 3), ringed(block, 0, 2)], axis=0))
    parts = [p for half in line for p in [half] + [ringed(half, 1, k) for k in (1, 2, 3)]]
    near, column_tiles, parent_front, parent_tile = lax.optimization_barrier(
        (near, column_tiles, parent_front, parent_tile)
    )
    small = jnp.concatenate([column_tiles.reshape(-1), parent_front[:, 0], parent_tile])
    other = swap(small)
    mine_first = (col // 2) * 8 + (col % 2) * 4 + jnp.arange(4)
    blocks = jnp.concatenate([small[:32] // 2, other[:32] // 2, mine_first])
    dx = (x - (blocks // 16) * 2 - (blocks // 4) % 2) % 4
    dy = (y - blocks) % 4
    first, second = jnp.where(core == 0, dy, dx), jnp.where(core == 0, dx, dy)
    half = first // 2
    place = ((half * 4 + second) * 2 + (first + half) % 2) * 2 + (blocks // 8 + core) % 2
    odd = jnp.concatenate([small[:32], other[:32]]) % 2
    meta = jnp.concatenate(
        [place[:64] * 2 + odd, small[32:34], other[32:34], small[34:], other[34:]]
        + [place[64:], core[None]]
    ).astype(jnp.int32)
    out = pl.pallas_call(
        products_kernel,
        out_shape=jax.ShapeDtypeStruct((16, 104, LANES), F32),
        in_specs=[SMEM] + [pl.BlockSpec(memory_space=pl.ANY)] * 12,
        out_specs=VMEM,
        scratch_shapes=[
            pltpu.VMEM((8192, LANES), jnp.bfloat16),
            pltpu.VMEM((2, 128, 2048), jnp.bfloat16),
            pltpu.VMEM((2, 128, 2048), jnp.bfloat16),
            pltpu.VMEM((512, 1024), jnp.bfloat16),
            pltpu.VMEM((512, 1024), jnp.bfloat16),
            pltpu.SemaphoreType.DMA((12,)),
        ],
        compiler_params=PARAMS,
    )(meta, *parts, child0, child1, slab0, slab1)
    arrived = lax.all_to_all(out, PLANE, 0, 0, tiled=True)
    labels = arrived[:, 96, :8].astype(jnp.int32)
    turned = (core == 1) & (jnp.arange(8) < 4)
    labels = jnp.where(turned, 7 - labels, labels)
    coded, direct = pl.pallas_call(
        combine_kernel,
        out_shape=(
            jax.ShapeDtypeStruct((8, 144, LANES), jnp.int16),
            jax.ShapeDtypeStruct((128, LANES), F32),
        ),
        in_specs=[SMEM, VMEM],
        out_specs=(VMEM, VMEM),
        scratch_shapes=[pltpu.VMEM((8, 128, LANES), F32)],
        compiler_params=PARAMS,
    )(labels, arrived)
    groups = [
        [z * 32 + n for z in (range(8) if n // 8 % 2 == 0 else range(7, -1, -1))]
        for n in range(32)
    ]
    pieces = lax.all_to_all(
        coded, ("z",) + CORES, 0, 0, tiled=True, axis_index_groups=groups
    )
    copies = pl.pallas_call(
        spread_kernel,
        out_shape=jax.ShapeDtypeStruct((32, 32, LANES), F32),
        in_specs=[VMEM, VMEM],
        out_specs=VMEM,
        compiler_params=PARAMS,
    )(pieces, direct)
    leaf = lax.all_to_all(copies, CORES, 0, 0, tiled=True)
    sampled, bases = pl.pallas_call(
        bases_kernel,
        out_shape=(
            jax.ShapeDtypeStruct((64, 256), F32),
            jax.ShapeDtypeStruct((64, 256), F32),
        ),
        in_specs=[SMEM, VMEM],
        out_specs=(VMEM, VMEM),
        scratch_shapes=[pltpu.VMEM((256, 384), F32)],
        compiler_params=PARAMS,
    )(jnp.stack([ranks[0, 0], col]).astype(jnp.int32), leaf.reshape(2, 2, 8, 4, 8, LANES))
    return sampled[None], bases[None]


def solution(mesh):
    split = Mesh(
        np.asarray(mesh.devices).reshape(8, 2, 2, 2, 4), ("z", "xh", "core", "xl", "y")
    )
    row, col = ("xh", "core"), ("xl", "y")
    in_specs = (
        P("z", row, col),
        P(row + col, None),
        P(("z",) + row + col, None, None),
        P(("z",) + row + col, None),
        P(("z",) + row + col),
        P(("z",) + row + col, None),
        P("z", row),
    )
    out_specs = (P("z", row + col, None), P("z", row + col, None))
    return jax.shard_map(
        on_device, mesh=split, in_specs=in_specs, out_specs=out_specs, check_vma=False
    )
```

```python
import jax
import jax.numpy as jnp
import numpy as np
from jax import lax
from jax.experimental import pallas as pl
from jax.experimental.pallas import tpu as pltpu
from jax.sharding import Mesh, PartitionSpec as P

F32 = jnp.float32
PLANE = ("xh", "xl", "y")
CORES = ("xh", "core", "xl", "y")
VMEM = pl.BlockSpec(memory_space=pltpu.VMEM)
SMEM = pl.BlockSpec(memory_space=pltpu.SMEM)
PARAMS = pltpu.CompilerParams(vmem_limit_bytes=50 * 1024 * 1024)
LANES = 128


def products_kernel(
    meta, part0, part1, part2, part3, child0, child1, slab0, slab1, out, omega
):
    for n, part in enumerate((part0, part1, part2, part3)):
        omega[2048 * n : 2048 * n + 2048, :] = part[...]
    lane = lax.broadcasted_iota(jnp.int32, (8, LANES), 1)
    label = jnp.zeros((8, LANES), jnp.int32)
    for n in range(8):
        label = jnp.where(lane == n, meta[64 + n], label)
    out[:, 96:104, :] = jnp.broadcast_to(label.astype(F32)[None], (16, 8, LANES))
    for t in range(4):
        child = (child0, child1)[t // 2]
        acc = jnp.zeros((128, LANES), F32)
        for b in range(0, 16, 2):
            one = omega[pl.ds(pl.multiple_of(meta[16 * t + b] * 128, 128), 128), :]
            two = omega[pl.ds(pl.multiple_of(meta[16 * t + b + 1] * 128, 128), 128), :]
            acc += jnp.dot(
                child[t % 2, :, 128 * b : 128 * b + 256],
                jnp.concatenate([one, two], axis=0),
                preferred_element_type=F32,
            )
        out[:, 8 * t : 8 * t + 8, :] = acc.reshape(16, 8, LANES)
    own = jnp.concatenate(
        [omega[pl.ds(pl.multiple_of(meta[72 + b] * 256, 256), 256), :] for b in range(4)], axis=0
    )
    core = meta[76]
    for o, slab in enumerate((slab0, slab1)):
        half = core if o == 0 else 1 - core
        acc = jnp.dot(slab[...], own, preferred_element_type=F32).reshape(4, 16, 8, LANES)
        for q in range(4):
            start = pl.multiple_of(32 + half * 32 + 8 * q, 8)
            out[:, pl.ds(start, 8), :] = acc[q]


def combine_kernel(labels, arrived, coded, direct, extended):
    extended[...] = jnp.zeros(extended.shape, F32)
    for s in range(16):
        for t in range(4):
            start = pl.multiple_of(labels[s, 4 + t] * 8, 8)
            extended[labels[s, t], pl.ds(start, 8), :] += arrived[s, 8 * t : 8 * t + 8, :]
    for p in range(8):
        value = extended[p].reshape(16, 8, LANES)
        top = jnp.maximum(jnp.max(jnp.abs(value), axis=1), 1e-30)
        power = jnp.floor(jnp.log2(top)) + 1.0
        scaled = jnp.round(value * jnp.exp2(15.0 - power)[:, None, :])
        scaled = jnp.clip(scaled, -32767.0, 32767.0).reshape(128, LANES)
        coded[p, :128, :] = scaled.astype(jnp.int32).astype(jnp.int16)
        coded[p, 128:, :] = power.astype(jnp.int32).astype(jnp.int16)
    for xh in range(2):
        total = arrived[8 * xh, 32:96, :]
        for c in range(1, 8):
            total += arrived[8 * xh + c, 32:96, :]
        direct[64 * xh : 64 * xh + 64, :] = total


def spread_kernel(pieces, direct, out):
    total = direct[...].reshape(16, 8, LANES)
    for z in range(8):
        power = pieces[z, 128:, :].astype(jnp.int32).astype(F32)
        value = pieces[z, :128, :].astype(jnp.int32).astype(F32).reshape(16, 8, LANES)
        total += value * jnp.exp2(power - 15.0)[:, None, :]
    total = total.reshape(4, 32, LANES)
    for n in range(4):
        for c in range(8):
            out[8 * n + c] = total[n]


def exact_dot(a, b):
    return lax.dot_general(
        a, b, (((0,), (0,)), ((), ())),
        precision=lax.Precision.HIGHEST, preferred_element_type=F32,
    )


def eliminated(panel, at, width, group):
    done = []
    wide = panel.shape[1] // LANES
    for g in range(0, width, group):
        rows = panel.shape[0]
        row = lax.broadcasted_iota(jnp.int32, (rows, LANES), 0)
        columns = [
            jnp.broadcast_to(panel[:, at + g + t : at + g + t + 1], (rows, LANES))
            for t in range(group)
        ]
        for t in range(group):
            pivot_row = panel[t : t + 1, :]
            pivot = columns[t][t : t + 1, :]
            factor = jnp.where(row > t, columns[t] * (1.0 / pivot), 0.0)
            done.append(pivot_row * jnp.concatenate([lax.rsqrt(pivot)] * wide, axis=1))
            for u in range(t + 1, group):
                columns[u] = columns[u] - factor * columns[u][t : t + 1, :]
            panel = panel - jnp.concatenate([factor] * wide, axis=1) * pivot_row
        panel = panel[group:, :]
    return jnp.concatenate(done, axis=0)


def bases_kernel(meta, leaf, sampled, bases, aug):
    rank, at = meta[0], meta[1]
    n = 256
    keep = lax.broadcasted_iota(jnp.int32, (1, n), 1) < rank
    own = jnp.concatenate(
        [leaf[at % 2, k, :, at // 2].reshape(64, LANES) for k in range(2)], axis=1
    )
    sampled[...] = own
    full = jnp.concatenate([leaf[:, k].reshape(512, LANES) for k in range(2)], axis=1)
    masked = jnp.where(keep, full, 0.0)
    r = lax.broadcasted_iota(jnp.int32, (n, n), 0)
    c = lax.broadcasted_iota(jnp.int32, (n, n), 1)
    aug[:, :n] = exact_dot(masked, masked) + jnp.where((r == c) & (c >= rank), 1.0, 0.0)
    mine = jnp.where(keep, own, 0.0)
    aug[:, n:] = jnp.concatenate([mine.T, jnp.zeros((n, 64), F32)], axis=1)
    width = 64
    for base in range(0, n, width):
        cut = base // LANES * LANES
        rest = base + width
        panel = eliminated(aug[base:rest, cut:], base - cut, width, 16)
        aug[base:rest, cut:] = panel
        if rest < n:
            low = rest // LANES * LANES
            tail = panel[:, low - cut :]
            update = exact_dot(tail[:, : n - low], tail)
            aug[rest:, low:] = aug[rest:, low:] - update[rest - low :, :]
    bases[...] = aug[:, n : n + 64].T


def ringed(v, stage, shift):
    pairs = []
    for n in range(32):
        xh, core, xl, y = n // 16, n // 8 % 2, n // 4 % 2, n % 4
        x = xh * 2 + xl
        if core == stage:
            y = (y + shift) % 4
        else:
            x = (x + shift) % 4
        pairs.append((n, ((x // 2 * 2 + core) * 2 + x % 2) * 4 + y))
    return lax.ppermute(v, CORES, pairs)


def on_device(front_slab, samples, child_tiles, parent_front, parent_tile, column_tiles, ranks):
    core, xh, xl, y = (lax.axis_index(name) for name in ("core", "xh", "xl", "y"))
    col, x = xl * 4 + y, xh * 2 + xl
    swap = lambda v: lax.ppermute(v, "core", [(0, 1), (1, 0)])
    left, right = samples[:, :LANES], samples[:, LANES:]
    mine = jnp.where(core == 0, left, right)
    block = jnp.concatenate([mine, swap(jnp.where(core == 0, right, left))], axis=0)
    child0, slab0 = child_tiles, front_slab[0]
    child1, slab1 = swap(child0), swap(slab0)
    line = jnp.concatenate([block] + [ringed(block, 0, k) for k in (1, 2, 3)], axis=0)
    parts = [line] + [ringed(line, 1, k) for k in (1, 2, 3)]
    parts[1], column_tiles, parent_front, parent_tile = lax.optimization_barrier(
        (parts[1], column_tiles, parent_front, parent_tile)
    )
    small = jnp.concatenate([column_tiles.reshape(-1), parent_front[:, 0], parent_tile])
    other = swap(small)
    mine_first = (col // 2) * 8 + (col % 2) * 4 + jnp.arange(4)
    blocks = jnp.concatenate([small[:32] // 2, other[:32] // 2, mine_first])
    dx = (x - (blocks // 16) * 2 - (blocks // 4) % 2) % 4
    dy = (y - blocks) % 4
    first, second = jnp.where(core == 0, dy, dx), jnp.where(core == 0, dx, dy)
    place = (second * 4 + first) * 2 + (blocks // 8 + core) % 2
    odd = jnp.concatenate([small[:32], other[:32]]) % 2
    meta = jnp.concatenate(
        [place[:64] * 2 + odd, small[32:34], other[32:34], small[34:], other[34:]]
        + [place[64:], core[None]]
    ).astype(jnp.int32)
    out = pl.pallas_call(
        products_kernel,
        out_shape=jax.ShapeDtypeStruct((16, 104, LANES), F32),
        in_specs=[SMEM] + [VMEM] * 8,
        out_specs=VMEM,
        scratch_shapes=[pltpu.VMEM((8192, LANES), jnp.bfloat16)],
        compiler_params=PARAMS,
    )(meta, *parts, child0, child1, slab0, slab1)
    arrived = lax.all_to_all(out, PLANE, 0, 0, tiled=True)
    labels = arrived[:, 96, :8].astype(jnp.int32)
    turned = (core == 1) & (jnp.arange(8) < 4)
    labels = jnp.where(turned, 7 - labels, labels)
    coded, direct = pl.pallas_call(
        combine_kernel,
        out_shape=(
            jax.ShapeDtypeStruct((8, 144, LANES), jnp.int16),
            jax.ShapeDtypeStruct((128, LANES), F32),
        ),
        in_specs=[SMEM, VMEM],
        out_specs=(VMEM, VMEM),
        scratch_shapes=[pltpu.VMEM((8, 128, LANES), F32)],
        compiler_params=PARAMS,
    )(labels, arrived)
    groups = [
        [z * 32 + n for z in (range(8) if n // 8 % 2 == 0 else range(7, -1, -1))]
        for n in range(32)
    ]
    pieces = lax.all_to_all(
        coded, ("z",) + CORES, 0, 0, tiled=True, axis_index_groups=groups
    )
    copies = pl.pallas_call(
        spread_kernel,
        out_shape=jax.ShapeDtypeStruct((32, 32, LANES), F32),
        in_specs=[VMEM, VMEM],
        out_specs=VMEM,
        compiler_params=PARAMS,
    )(pieces, direct)
    leaf = lax.all_to_all(copies, CORES, 0, 0, tiled=True)
    sampled, bases = pl.pallas_call(
        bases_kernel,
        out_shape=(
            jax.ShapeDtypeStruct((64, 256), F32),
            jax.ShapeDtypeStruct((64, 256), F32),
        ),
        in_specs=[SMEM, VMEM],
        out_specs=(VMEM, VMEM),
        scratch_shapes=[pltpu.VMEM((256, 384), F32)],
        compiler_params=PARAMS,
    )(jnp.stack([ranks[0, 0], col]).astype(jnp.int32), leaf.reshape(2, 2, 8, 4, 8, LANES))
    return sampled[None], bases[None]


def solution(mesh):
    split = Mesh(
        np.asarray(mesh.devices).reshape(8, 2, 2, 2, 4), ("z", "xh", "core", "xl", "y")
    )
    row, col = ("xh", "core"), ("xl", "y")
    in_specs = (
        P("z", row, col),
        P(row + col, None),
        P(("z",) + row + col, None, None),
        P(("z",) + row + col, None),
        P(("z",) + row + col),
        P(("z",) + row + col, None),
        P("z", row),
    )
    out_specs = (P("z", row + col, None), P("z", row + col, None))
    return jax.shard_map(
        on_device, mesh=split, in_specs=in_specs, out_specs=out_specs, check_vma=False
    )
```

```python
import jax
import jax.numpy as jnp
import numpy as np
from jax import lax
from jax.experimental import pallas as pl
from jax.experimental.pallas import tpu as pltpu
from jax.sharding import Mesh, PartitionSpec as P

F32 = jnp.float32
PLANE = ("xh", "xl", "y")
CORES = ("xh", "core", "xl", "y")
VMEM = pl.BlockSpec(memory_space=pltpu.VMEM)
SMEM = pl.BlockSpec(memory_space=pltpu.SMEM)
PARAMS = pltpu.CompilerParams(vmem_limit_bytes=50 * 1024 * 1024)
LANES = 128


def exponents(value):
    top = jnp.maximum(jnp.max(jnp.abs(value), axis=1, keepdims=True), 1e-30)
    return jnp.floor(jnp.log2(top)) + 1.0


def coded_as(value, power):
    scaled = jnp.round(value * jnp.exp2(15.0 - power))
    return jnp.clip(scaled, -32767.0, 32767.0).astype(jnp.int32)


def plain(coded):
    return coded.astype(jnp.int32).astype(F32)


def products_kernel(
    meta, part0, part1, part2, part3, child0, child1_in, slab0_in, slab1_in,
    out, omega, child1, slab0, slab1, sems,
):
    copies = [
        pltpu.make_async_copy(source, target, sems.at[n])
        for n, (source, target) in enumerate(
            ((child1_in, child1), (slab0_in, slab0), (slab1_in, slab1))
        )
    ]
    for copy in copies:
        copy.start()
    for n, part in enumerate((part0, part1, part2, part3)):
        omega[2048 * n : 2048 * n + 2048, :] = part[...]
    core = meta[76]
    rows = lax.broadcasted_iota(jnp.int32, (16, LANES), 0)
    lane = lax.broadcasted_iota(jnp.int32, (16, LANES), 1)
    tail = jnp.zeros((16, LANES), jnp.int32)
    for n in range(8):
        tail = jnp.where((rows == 12) & (lane == n), meta[64 + n], tail)

    def kept(tiles, start, tail, first):
        value = jnp.stack(tiles)
        power = exponents(value)
        code = coded_as(value, power).reshape(2, 16, 8, LANES)
        pair = jnp.concatenate([code[0], code[1]], axis=1)
        out[:, pl.ds(pl.multiple_of(start, 16), 16), :] = pair.astype(jnp.int16)
        for n in range(2):
            tail = jnp.where(rows == first + n, power[n].astype(jnp.int32), tail)
        return tail

    for pair in range(2):
        child = (child0, child1)[pair]
        if pair == 1:
            copies[0].wait()
        tiles = []
        for t in range(2):
            acc = jnp.zeros((128, LANES), F32)
            for b in range(0, 16, 2):
                at = 32 * pair + 16 * t + b
                one = omega[pl.ds(pl.multiple_of(meta[at] * 128, 128), 128), :]
                two = omega[pl.ds(pl.multiple_of(meta[at + 1] * 128, 128), 128), :]
                acc += jnp.dot(
                    child[t, :, 128 * b : 128 * b + 256],
                    jnp.concatenate([one, two], axis=0),
                    preferred_element_type=F32,
                )
            tiles.append(acc)
        tail = kept(tiles, 16 * pair, tail, 2 * pair)
    own = jnp.concatenate(
        [omega[pl.ds(pl.multiple_of(meta[72 + b] * 256, 256), 256), :] for b in range(4)], axis=0
    )
    for o, slab in enumerate((slab0, slab1)):
        copies[1 + o].wait()
        half = core if o == 0 else 1 - core
        acc = jnp.dot(slab[...], own, preferred_element_type=F32).reshape(4, 128, LANES)
        for q in (0, 2):
            tail = kept([acc[q], acc[q + 1]], 32 + 32 * half + 8 * q, tail, 4 + 4 * half + q)
    out[:, 96:112, :] = jnp.broadcast_to(tail[None], (16, 16, LANES)).astype(jnp.int16)


def combine_kernel(labels, arrived, coded, direct, extended):
    extended[...] = jnp.zeros(extended.shape, F32)
    totals = []
    for s in range(16):
        scale = jnp.exp2(plain(arrived[s, 96:112, :]) - 15.0)
        for t in range(4):
            value = plain(arrived[s, 16 * (t // 2) : 16 * (t // 2) + 16, :])
            value = value[8 * (t % 2) : 8 * (t % 2) + 8, :] * scale[t : t + 1, :]
            start = pl.multiple_of(labels[s, 4 + t] * 8, 8)
            extended[labels[s, t], pl.ds(start, 8), :] += value
        value = plain(arrived[s, 32:96, :]).reshape(8, 8, LANES) * scale[4:12, None, :]
        if s % 8 == 0:
            totals.append(value)
        else:
            totals[-1] += value
    for p in range(8):
        value = extended[p].reshape(16, 8, LANES)
        power = exponents(value)
        coded[p, :128, :] = coded_as(value, power).reshape(128, LANES).astype(jnp.int16)
        coded[p, 128:, :] = power[:, 0, :].astype(jnp.int32).astype(jnp.int16)
    for xh in range(2):
        direct[64 * xh : 64 * xh + 64, :] = totals[xh].reshape(64, LANES)


def spread_kernel(pieces, direct, out):
    total = direct[...].reshape(16, 8, LANES)
    for z in range(8):
        power = plain(pieces[z, 128:, :])
        value = plain(pieces[z, :128, :]).reshape(16, 8, LANES)
        total += value * jnp.exp2(power - 15.0)[:, None, :]
    total = total.reshape(4, 32, LANES)
    for n in range(4):
        for c in range(8):
            out[8 * n + c] = total[n]


def exact_dot(a, b):
    return lax.dot_general(
        a, b, (((0,), (0,)), ((), ())),
        precision=lax.Precision.HIGHEST, preferred_element_type=F32,
    )


def eliminated(panel, at, width, group):
    done = []
    wide = panel.shape[1] // LANES
    for g in range(0, width, group):
        rows = panel.shape[0]
        row = lax.broadcasted_iota(jnp.int32, (rows, LANES), 0)
        columns = [
            jnp.broadcast_to(panel[:, at + g + t : at + g + t + 1], (rows, LANES))
            for t in range(group)
        ]
        for t in range(group):
            pivot_row = panel[t : t + 1, :]
            pivot = columns[t][t : t + 1, :]
            factor = jnp.where(row > t, columns[t] * (1.0 / pivot), 0.0)
            done.append(pivot_row * jnp.concatenate([lax.rsqrt(pivot)] * wide, axis=1))
            for u in range(t + 1, group):
                columns[u] = columns[u] - factor * columns[u][t : t + 1, :]
            panel = panel - jnp.concatenate([factor] * wide, axis=1) * pivot_row
        panel = panel[group:, :]
    return jnp.concatenate(done, axis=0)


def bases_kernel(meta, leaf, sampled, bases, aug):
    rank, at = meta[0], meta[1]
    n = 256
    keep = lax.broadcasted_iota(jnp.int32, (1, n), 1) < rank
    own = jnp.concatenate(
        [leaf[at % 2, k, :, at // 2].reshape(64, LANES) for k in range(2)], axis=1
    )
    sampled[...] = own
    full = jnp.concatenate([leaf[:, k].reshape(512, LANES) for k in range(2)], axis=1)
    masked = jnp.where(keep, full, 0.0)
    r = lax.broadcasted_iota(jnp.int32, (n, n), 0)
    c = lax.broadcasted_iota(jnp.int32, (n, n), 1)
    aug[:, :n] = exact_dot(masked, masked) + jnp.where((r == c) & (c >= rank), 1.0, 0.0)
    mine = jnp.where(keep, own, 0.0)
    aug[:, n:] = jnp.concatenate([mine.T, jnp.zeros((n, 64), F32)], axis=1)
    width = 64
    for base in range(0, n, width):
        cut = base // LANES * LANES
        rest = base + width
        panel = eliminated(aug[base:rest, cut:], base - cut, width, 16)
        aug[base:rest, cut:] = panel
        if rest < n:
            low = rest // LANES * LANES
            tail = panel[:, low - cut :]
            update = exact_dot(tail[:, : n - low], tail)
            aug[rest:, low:] = aug[rest:, low:] - update[rest - low :, :]
    bases[...] = aug[:, n : n + 64].T


def ringed(v, stage, shift):
    pairs = []
    for n in range(32):
        xh, core, xl, y = n // 16, n // 8 % 2, n // 4 % 2, n % 4
        x = xh * 2 + xl
        if core == stage:
            y = (y + shift) % 4
        else:
            x = (x + shift) % 4
        pairs.append((n, ((x // 2 * 2 + core) * 2 + x % 2) * 4 + y))
    return lax.ppermute(v, CORES, pairs)


def on_device(front_slab, samples, child_tiles, parent_front, parent_tile, column_tiles, ranks):
    core, xh, xl, y = (lax.axis_index(name) for name in ("core", "xh", "xl", "y"))
    col, x = xl * 4 + y, xh * 2 + xl
    swap = lambda v: lax.ppermute(v, "core", [(0, 1), (1, 0)])
    left, right = samples[:, :LANES], samples[:, LANES:]
    mine = jnp.where(core == 0, left, right)
    block = jnp.concatenate([mine, swap(jnp.where(core == 0, right, left))], axis=0)
    child0, slab0 = child_tiles, front_slab[0]
    child1, slab1 = swap(child0), swap(slab0)
    line = jnp.concatenate([block] + [ringed(block, 0, k) for k in (1, 2, 3)], axis=0)
    parts = [line] + [ringed(line, 1, k) for k in (1, 2, 3)]
    parts[1], column_tiles, parent_front, parent_tile = lax.optimization_barrier(
        (parts[1], column_tiles, parent_front, parent_tile)
    )
    small = jnp.concatenate([column_tiles.reshape(-1), parent_front[:, 0], parent_tile])
    other = swap(small)
    mine_first = (col // 2) * 8 + (col % 2) * 4 + jnp.arange(4)
    blocks = jnp.concatenate([small[:32] // 2, other[:32] // 2, mine_first])
    dx = (x - (blocks // 16) * 2 - (blocks // 4) % 2) % 4
    dy = (y - blocks) % 4
    first, second = jnp.where(core == 0, dy, dx), jnp.where(core == 0, dx, dy)
    place = (second * 4 + first) * 2 + (blocks // 8 + core) % 2
    odd = jnp.concatenate([small[:32], other[:32]]) % 2
    meta = jnp.concatenate(
        [place[:64] * 2 + odd, small[32:34], other[32:34], small[34:], other[34:]]
        + [place[64:], core[None]]
    ).astype(jnp.int32)
    out = pl.pallas_call(
        products_kernel,
        out_shape=jax.ShapeDtypeStruct((16, 112, LANES), jnp.int16),
        in_specs=[SMEM] + [VMEM] * 5 + [pl.BlockSpec(memory_space=pl.ANY)] * 3,
        out_specs=VMEM,
        scratch_shapes=[
            pltpu.VMEM((8192, LANES), jnp.bfloat16),
            pltpu.VMEM((2, 128, 2048), jnp.bfloat16),
            pltpu.VMEM((512, 1024), jnp.bfloat16),
            pltpu.VMEM((512, 1024), jnp.bfloat16),
            pltpu.SemaphoreType.DMA((3,)),
        ],
        compiler_params=PARAMS,
    )(meta, *parts, child0, child1, slab0, slab1)
    arrived = lax.all_to_all(out, PLANE, 0, 0, tiled=True)
    labels = arrived[:, 108, :8].astype(jnp.int32)
    turned = (core == 1) & (jnp.arange(8) < 4)
    labels = jnp.where(turned, 7 - labels, labels)
    coded, direct = pl.pallas_call(
        combine_kernel,
        out_shape=(
            jax.ShapeDtypeStruct((8, 144, LANES), jnp.int16),
            jax.ShapeDtypeStruct((128, LANES), F32),
        ),
        in_specs=[SMEM, VMEM],
        out_specs=(VMEM, VMEM),
        scratch_shapes=[pltpu.VMEM((8, 128, LANES), F32)],
        compiler_params=PARAMS,
    )(labels, arrived)
    groups = [
        [z * 32 + n for z in (range(8) if n // 8 % 2 == 0 else range(7, -1, -1))]
        for n in range(32)
    ]
    pieces = lax.all_to_all(
        coded, ("z",) + CORES, 0, 0, tiled=True, axis_index_groups=groups
    )
    copies = pl.pallas_call(
        spread_kernel,
        out_shape=jax.ShapeDtypeStruct((32, 32, LANES), F32),
        in_specs=[VMEM, VMEM],
        out_specs=VMEM,
        compiler_params=PARAMS,
    )(pieces, direct)
    leaf = lax.all_to_all(copies, CORES, 0, 0, tiled=True)
    sampled, bases = pl.pallas_call(
        bases_kernel,
        out_shape=(
            jax.ShapeDtypeStruct((64, 256), F32),
            jax.ShapeDtypeStruct((64, 256), F32),
        ),
        in_specs=[SMEM, VMEM],
        out_specs=(VMEM, VMEM),
        scratch_shapes=[pltpu.VMEM((256, 384), F32)],
        compiler_params=PARAMS,
    )(jnp.stack([ranks[0, 0], col]).astype(jnp.int32), leaf.reshape(2, 2, 8, 4, 8, LANES))
    return sampled[None], bases[None]


def solution(mesh):
    split = Mesh(
        np.asarray(mesh.devices).reshape(8, 2, 2, 2, 4), ("z", "xh", "core", "xl", "y")
    )
    row, col = ("xh", "core"), ("xl", "y")
    in_specs = (
        P("z", row, col),
        P(row + col, None),
        P(("z",) + row + col, None, None),
        P(("z",) + row + col, None),
        P(("z",) + row + col),
        P(("z",) + row + col, None),
        P("z", row),
    )
    out_specs = (P("z", row + col, None), P("z", row + col, None))
    return jax.shard_map(
        on_device, mesh=split, in_specs=in_specs, out_specs=out_specs, check_vma=False
    )
```

```python
import jax
import jax.numpy as jnp
import numpy as np
from jax import lax
from jax.experimental import pallas as pl
from jax.experimental.pallas import tpu as pltpu
from jax.sharding import Mesh, PartitionSpec as P

F32 = jnp.float32
PLANE = ("xh", "xl", "y")
CORES = ("xh", "core", "xl", "y")
VMEM = pl.BlockSpec(memory_space=pltpu.VMEM)
SMEM = pl.BlockSpec(memory_space=pltpu.SMEM)
SMALL = pltpu.CompilerParams(vmem_limit_bytes=16 * 1024 * 1024)
PARAMS = pltpu.CompilerParams(vmem_limit_bytes=50 * 1024 * 1024)
LANES = 128


def exponents(value):
    top = jnp.maximum(jnp.max(jnp.abs(value), axis=1, keepdims=True), 1e-30)
    return jnp.floor(jnp.log2(top)) + 1.0


def coded_as(value, power):
    scaled = jnp.round(value * jnp.exp2(15.0 - power))
    return jnp.clip(scaled, -32767.0, 32767.0).astype(jnp.int32)


def plain(coded):
    return coded.astype(jnp.int32).astype(F32)


def products_kernel(
    meta, part0, part1, part2, part3, child0, child1_in, slab0_in, slab1_in,
    out, omega, child1, slab0, slab1, sems,
):
    copies = [
        pltpu.make_async_copy(source, target, sems.at[n])
        for n, (source, target) in enumerate(
            ((child1_in, child1), (slab0_in, slab0), (slab1_in, slab1))
        )
    ]
    for copy in copies:
        copy.start()
    for n, part in enumerate((part0, part1, part2, part3)):
        omega[2048 * n : 2048 * n + 2048, :] = part[...]
    core = meta[76]
    rows = lax.broadcasted_iota(jnp.int32, (16, LANES), 0)
    lane = lax.broadcasted_iota(jnp.int32, (16, LANES), 1)
    tail = jnp.zeros((16, LANES), jnp.int32)
    for n in range(8):
        tail = jnp.where((rows == 12) & (lane == n), meta[64 + n], tail)

    def kept(tiles, start, tail, first):
        value = jnp.stack(tiles)
        power = exponents(value)
        code = coded_as(value, power).reshape(2, 16, 8, LANES)
        pair = jnp.concatenate([code[0], code[1]], axis=1)
        out[:, pl.ds(pl.multiple_of(start, 16), 16), :] = pair.astype(jnp.int16)
        for n in range(2):
            tail = jnp.where(rows == first + n, power[n].astype(jnp.int32), tail)
        return tail

    for pair in range(2):
        child = (child0, child1)[pair]
        if pair == 1:
            copies[0].wait()
        tiles = []
        for t in range(2):
            acc = jnp.zeros((128, LANES), F32)
            for b in range(0, 16, 2):
                at = 32 * pair + 16 * t + b
                one = omega[pl.ds(pl.multiple_of(meta[at] * 128, 128), 128), :]
                two = omega[pl.ds(pl.multiple_of(meta[at + 1] * 128, 128), 128), :]
                acc += jnp.dot(
                    child[t, :, 128 * b : 128 * b + 256],
                    jnp.concatenate([one, two], axis=0),
                    preferred_element_type=F32,
                )
            tiles.append(acc)
        tail = kept(tiles, 16 * pair, tail, 2 * pair)
    own = jnp.concatenate(
        [omega[pl.ds(pl.multiple_of(meta[72 + b] * 256, 256), 256), :] for b in range(4)], axis=0
    )
    for o, slab in enumerate((slab0, slab1)):
        copies[1 + o].wait()
        half = core if o == 0 else 1 - core
        acc = jnp.dot(slab[...], own, preferred_element_type=F32).reshape(4, 128, LANES)
        for q in (0, 2):
            tail = kept([acc[q], acc[q + 1]], 32 + 32 * half + 8 * q, tail, 4 + 4 * half + q)
    out[:, 96:112, :] = jnp.broadcast_to(tail[None], (16, 16, LANES)).astype(jnp.int16)


def combine_kernel(labels, arrived, coded, direct, extended):
    extended[...] = jnp.zeros(extended.shape, F32)
    totals = []
    for s in range(16):
        scale = jnp.exp2(plain(arrived[s, 96:112, :]) - 15.0)
        for t in range(4):
            value = plain(arrived[s, 16 * (t // 2) : 16 * (t // 2) + 16, :])
            value = value[8 * (t % 2) : 8 * (t % 2) + 8, :] * scale[t : t + 1, :]
            start = pl.multiple_of(labels[s, 4 + t] * 8, 8)
            extended[labels[s, t], pl.ds(start, 8), :] += value
        value = plain(arrived[s, 32:96, :]).reshape(8, 8, LANES) * scale[4:12, None, :]
        if s % 8 == 0:
            totals.append(value)
        else:
            totals[-1] += value
    for p in range(8):
        value = extended[p].reshape(16, 8, LANES)
        power = exponents(value)
        coded[p, :128, :] = coded_as(value, power).reshape(128, LANES).astype(jnp.int16)
        coded[p, 128:, :] = power[:, 0, :].astype(jnp.int32).astype(jnp.int16)
    for xh in range(2):
        direct[64 * xh : 64 * xh + 64, :] = totals[xh].reshape(64, LANES)


def spread_kernel(pieces, direct, out):
    total = direct[...].reshape(16, 8, LANES)
    for z in range(8):
        power = plain(pieces[z, 128:, :])
        value = plain(pieces[z, :128, :]).reshape(16, 8, LANES)
        total += value * jnp.exp2(power - 15.0)[:, None, :]
    total = total.reshape(4, 32, LANES)
    power = exponents(total)
    code = coded_as(total, power)
    power = jnp.broadcast_to(power, (4, 8, LANES)).astype(jnp.int32)
    block = jnp.concatenate([code, power], axis=1).astype(jnp.int16)
    for n in range(4):
        for c in range(8):
            out[8 * n + c] = block[n]


def exact_dot(a, b):
    return lax.dot_general(
        a, b, (((0,), (0,)), ((), ())),
        precision=lax.Precision.HIGHEST, preferred_element_type=F32,
    )


def eliminated(panel, at, width, group):
    done = []
    wide = panel.shape[1] // LANES
    for g in range(0, width, group):
        rows = panel.shape[0]
        row = lax.broadcasted_iota(jnp.int32, (rows, LANES), 0)
        columns = [
            jnp.broadcast_to(panel[:, at + g + t : at + g + t + 1], (rows, LANES))
            for t in range(group)
        ]
        for t in range(group):
            pivot_row = panel[t : t + 1, :]
            pivot = columns[t][t : t + 1, :]
            factor = jnp.where(row > t, columns[t] * (1.0 / pivot), 0.0)
            done.append(pivot_row * jnp.concatenate([lax.rsqrt(pivot)] * wide, axis=1))
            for u in range(t + 1, group):
                columns[u] = columns[u] - factor * columns[u][t : t + 1, :]
            panel = panel - jnp.concatenate([factor] * wide, axis=1) * pivot_row
        panel = panel[group:, :]
    return jnp.concatenate(done, axis=0)


def bases_kernel(meta, arrived, sampled, bases, aug, leaf):
    rank, at = meta[0], meta[1]
    for xh in range(2):
        for k in range(2):
            block = plain(arrived[xh, k])
            leaf[xh, k] = block[:, :32, :] * jnp.exp2(block[:, 32:33, :] - 15.0)
    rows = pl.multiple_of(at // 2 * 8, 8)
    n = 256
    keep = lax.broadcasted_iota(jnp.int32, (1, n), 1) < rank
    own = jnp.concatenate(
        [leaf[at % 2, k, :, pl.ds(rows, 8), :].reshape(64, LANES) for k in range(2)], axis=1
    )
    sampled[...] = own
    full = jnp.concatenate([leaf[:, k].reshape(512, LANES) for k in range(2)], axis=1)
    masked = jnp.where(keep, full, 0.0)
    r = lax.broadcasted_iota(jnp.int32, (n, n), 0)
    c = lax.broadcasted_iota(jnp.int32, (n, n), 1)
    aug[:, :n] = exact_dot(masked, masked) + jnp.where((r == c) & (c >= rank), 1.0, 0.0)
    mine = jnp.where(keep, own, 0.0)
    aug[:, n:] = jnp.concatenate([mine.T, jnp.zeros((n, 64), F32)], axis=1)
    width = 64
    for base in range(0, n, width):
        cut = base // LANES * LANES
        rest = base + width
        panel = eliminated(aug[base:rest, cut:], base - cut, width, 16)
        aug[base:rest, cut:] = panel
        if rest < n:
            low = rest // LANES * LANES
            tail = panel[:, low - cut :]
            update = exact_dot(tail[:, : n - low], tail)
            aug[rest:, low:] = aug[rest:, low:] - update[rest - low :, :]
    bases[...] = aug[:, n : n + 64].T


def ringed(v, stage, shift):
    pairs = []
    for n in range(32):
        xh, core, xl, y = n // 16, n // 8 % 2, n // 4 % 2, n % 4
        x = xh * 2 + xl
        if core == stage:
            y = (y + shift) % 4
        else:
            x = (x + shift) % 4
        pairs.append((n, ((x // 2 * 2 + core) * 2 + x % 2) * 4 + y))
    return lax.ppermute(v, CORES, pairs)


def on_device(front_slab, samples, child_tiles, parent_front, parent_tile, column_tiles, ranks):
    core, xh, xl, y = (lax.axis_index(name) for name in ("core", "xh", "xl", "y"))
    col, x = xl * 4 + y, xh * 2 + xl
    swap = lambda v: lax.ppermute(v, "core", [(0, 1), (1, 0)])
    half = lambda v: jnp.where(core == 0, v[:, :LANES], v[:, LANES:])
    block = jnp.concatenate([half(samples), half(swap(samples))], axis=0)
    child0, slab0 = child_tiles, front_slab[0]
    child1, slab1 = swap(child0), swap(slab0)
    line = jnp.concatenate([block] + [ringed(block, 0, k) for k in (1, 2, 3)], axis=0)
    parts = [line] + [ringed(line, 1, k) for k in (1, 2, 3)]
    parts[1], column_tiles, parent_front, parent_tile = lax.optimization_barrier(
        (parts[1], column_tiles, parent_front, parent_tile)
    )
    small = jnp.concatenate([column_tiles.reshape(-1), parent_front[:, 0], parent_tile])
    other = swap(small)
    mine_first = (col // 2) * 8 + (col % 2) * 4 + jnp.arange(4)
    blocks = jnp.concatenate([small[:32] // 2, other[:32] // 2, mine_first])
    dx = (x - (blocks // 16) * 2 - (blocks // 4) % 2) % 4
    dy = (y - blocks) % 4
    first, second = jnp.where(core == 0, dy, dx), jnp.where(core == 0, dx, dy)
    place = (second * 4 + first) * 2 + (blocks // 8 + core) % 2
    odd = jnp.concatenate([small[:32], other[:32]]) % 2
    meta = jnp.concatenate(
        [place[:64] * 2 + odd, small[32:34], other[32:34], small[34:], other[34:]]
        + [place[64:], core[None]]
    ).astype(jnp.int32)
    out = pl.pallas_call(
        products_kernel,
        out_shape=jax.ShapeDtypeStruct((16, 112, LANES), jnp.int16),
        in_specs=[SMEM] + [VMEM] * 5 + [pl.BlockSpec(memory_space=pl.ANY)] * 3,
        out_specs=VMEM,
        scratch_shapes=[
            pltpu.VMEM((8192, LANES), jnp.bfloat16),
            pltpu.VMEM((2, 128, 2048), jnp.bfloat16),
            pltpu.VMEM((512, 1024), jnp.bfloat16),
            pltpu.VMEM((512, 1024), jnp.bfloat16),
            pltpu.SemaphoreType.DMA((3,)),
        ],
        compiler_params=PARAMS,
    )(meta, *parts, child0, child1, slab0, slab1)
    arrived = lax.all_to_all(out, PLANE, 0, 0, tiled=True)
    labels = arrived[:, 108, :8].astype(jnp.int32)
    turned = (core == 1) & (jnp.arange(8) < 4)
    labels = jnp.where(turned, 7 - labels, labels)
    coded, direct = pl.pallas_call(
        combine_kernel,
        out_shape=(
            jax.ShapeDtypeStruct((8, 144, LANES), jnp.int16),
            jax.ShapeDtypeStruct((128, LANES), F32),
        ),
        in_specs=[SMEM, VMEM],
        out_specs=(VMEM, VMEM),
        scratch_shapes=[pltpu.VMEM((8, 128, LANES), F32)],
        compiler_params=SMALL,
    )(labels, arrived)
    groups = [
        [z * 32 + n for z in (range(8) if n // 8 % 2 == 0 else range(7, -1, -1))]
        for n in range(32)
    ]
    pieces = lax.all_to_all(
        coded, ("z",) + CORES, 0, 0, tiled=True, axis_index_groups=groups
    )
    copies = pl.pallas_call(
        spread_kernel,
        out_shape=jax.ShapeDtypeStruct((32, 40, LANES), jnp.int16),
        in_specs=[VMEM, VMEM],
        out_specs=VMEM,
        compiler_params=SMALL,
    )(pieces, direct)
    leaf = lax.all_to_all(copies, CORES, 0, 0, tiled=True)
    sampled, bases = pl.pallas_call(
        bases_kernel,
        out_shape=(
            jax.ShapeDtypeStruct((64, 256), F32),
            jax.ShapeDtypeStruct((64, 256), F32),
        ),
        in_specs=[SMEM, VMEM],
        out_specs=(VMEM, VMEM),
        scratch_shapes=[
            pltpu.VMEM((256, 384), F32),
            pltpu.VMEM((2, 2, 8, 32, LANES), F32),
        ],
        compiler_params=SMALL,
    )(jnp.stack([ranks[0, 0], col]).astype(jnp.int32), leaf.reshape(2, 2, 8, 40, LANES))
    return sampled[None], bases[None]


def solution(mesh):
    split = Mesh(
        np.asarray(mesh.devices).reshape(8, 2, 2, 2, 4), ("z", "xh", "core", "xl", "y")
    )
    row, col = ("xh", "core"), ("xl", "y")
    in_specs = (
        P("z", row, col),
        P(row + col, None),
        P(("z",) + row + col, None, None),
        P(("z",) + row + col, None),
        P(("z",) + row + col),
        P(("z",) + row + col, None),
        P("z", row),
    )
    out_specs = (P("z", row + col, None), P("z", row + col, None))
    return jax.shard_map(
        on_device, mesh=split, in_specs=in_specs, out_specs=out_specs, check_vma=False
    )
```

```python
import jax
import jax.numpy as jnp
import numpy as np
from jax import lax
from jax.experimental import pallas as pl
from jax.experimental.pallas import tpu as pltpu
from jax.sharding import Mesh, PartitionSpec as P

F32 = jnp.float32
PLANE = ("xh", "xl", "y")
CORES = ("xh", "core", "xl", "y")
VMEM = pl.BlockSpec(memory_space=pltpu.VMEM)
SMEM = pl.BlockSpec(memory_space=pltpu.SMEM)
SMALL = pltpu.CompilerParams(vmem_limit_bytes=16 * 1024 * 1024)
PARAMS = pltpu.CompilerParams(vmem_limit_bytes=50 * 1024 * 1024)
LANES = 128


def exponents(value):
    top = jnp.maximum(jnp.max(jnp.abs(value), axis=1, keepdims=True), 1e-30)
    return jnp.floor(jnp.log2(top)) + 1.0


def coded_as(value, power):
    scaled = jnp.round(value * jnp.exp2(15.0 - power))
    return jnp.clip(scaled, -32767.0, 32767.0).astype(jnp.int32)


def plain(coded):
    return coded.astype(jnp.int32).astype(F32)


def products_kernel(
    meta, part0, part1, part2, part3, child0, child1_in, slab0_in, slab1_in,
    out, omega, child1, slab0, slab1, sems,
):
    copies = [
        pltpu.make_async_copy(source, target, sems.at[n])
        for n, (source, target) in enumerate(
            [(child1_in.at[t], child1.at[t]) for t in range(2)]
            + [
                (source.at[pl.ds(128 * t, 128)], target.at[pl.ds(128 * t, 128)])
                for source, target in ((slab0_in, slab0), (slab1_in, slab1))
                for t in range(4)
            ]
        )
    ]
    for copy in copies:
        copy.start()
    for n, part in enumerate((part0, part1, part2, part3)):
        omega[2048 * n : 2048 * n + 2048, :] = part[...]
    core = meta[76]
    rows = lax.broadcasted_iota(jnp.int32, (16, LANES), 0)
    lane = lax.broadcasted_iota(jnp.int32, (16, LANES), 1)
    tail = jnp.zeros((16, LANES), jnp.int32)
    for n in range(8):
        tail = jnp.where((rows == 12) & (lane == n), meta[64 + n], tail)

    def kept(tiles, start, tail, first):
        value = jnp.stack(tiles)
        power = exponents(value)
        code = coded_as(value, power).reshape(2, 16, 8, LANES)
        pair = jnp.concatenate([code[0], code[1]], axis=1)
        out[:, pl.ds(pl.multiple_of(start, 16), 16), :] = pair.astype(jnp.int16)
        for n in range(2):
            tail = jnp.where(rows == first + n, power[n].astype(jnp.int32), tail)
        return tail

    for pair in range(2):
        child = (child0, child1)[pair]
        tiles = []
        for t in range(2):
            if pair == 1:
                copies[t].wait()
            acc = jnp.zeros((128, LANES), F32)
            for b in range(0, 16, 2):
                at = 32 * pair + 16 * t + b
                one = omega[pl.ds(pl.multiple_of(meta[at] * 128, 128), 128), :]
                two = omega[pl.ds(pl.multiple_of(meta[at + 1] * 128, 128), 128), :]
                acc += jnp.dot(
                    child[t, :, 128 * b : 128 * b + 256],
                    jnp.concatenate([one, two], axis=0),
                    preferred_element_type=F32,
                )
            tiles.append(acc)
        tail = kept(tiles, 16 * pair, tail, 2 * pair)
    own = jnp.concatenate(
        [omega[pl.ds(pl.multiple_of(meta[72 + b] * 256, 256), 256), :] for b in range(4)], axis=0
    )
    for o, slab in enumerate((slab0, slab1)):
        for n in range(4):
            copies[2 + 4 * o + n].wait()
        half = core if o == 0 else 1 - core
        acc = jnp.dot(slab[...], own, preferred_element_type=F32).reshape(4, 128, LANES)
        for q in (0, 2):
            tail = kept([acc[q], acc[q + 1]], 32 + 32 * half + 8 * q, tail, 4 + 4 * half + q)
    out[:, 96:112, :] = jnp.broadcast_to(tail[None], (16, 16, LANES)).astype(jnp.int16)


def combine_kernel(labels, arrived, coded, direct, *sums):
    for part in sums:
        part[...] = jnp.zeros(part.shape, F32)
    totals = []
    for s in range(16):
        scale = jnp.exp2(plain(arrived[s, 96:112, :]) - 15.0)
        for t in range(4):
            value = plain(arrived[s, 16 * (t // 2) : 16 * (t // 2) + 16, :])
            value = value[8 * (t % 2) : 8 * (t % 2) + 8, :] * scale[t : t + 1, :]
            start = pl.multiple_of(labels[s, 4 + t] * 8, 8)
            sums[t][labels[s, t], pl.ds(start, 8), :] += value
        value = plain(arrived[s, 32:96, :]).reshape(8, 8, LANES) * scale[4:12, None, :]
        if s % 8 == 0:
            totals.append(value)
        else:
            totals[-1] += value
    for p in range(8):
        value = sum(part[p] for part in sums).reshape(16, 8, LANES)
        power = exponents(value)
        coded[p, :128, :] = coded_as(value, power).reshape(128, LANES).astype(jnp.int16)
        coded[p, 128:, :] = power[:, 0, :].astype(jnp.int32).astype(jnp.int16)
    for xh in range(2):
        direct[64 * xh : 64 * xh + 64, :] = totals[xh].reshape(64, LANES)


def spread_kernel(pieces, direct, out):
    total = direct[...].reshape(16, 8, LANES)
    for z in range(8):
        power = plain(pieces[z, 128:, :])
        value = plain(pieces[z, :128, :]).reshape(16, 8, LANES)
        total += value * jnp.exp2(power - 15.0)[:, None, :]
    total = total.reshape(4, 32, LANES)
    power = exponents(total)
    code = coded_as(total, power)
    power = jnp.broadcast_to(power, (4, 8, LANES)).astype(jnp.int32)
    block = jnp.concatenate([code, power], axis=1).astype(jnp.int16)
    for n in range(4):
        for c in range(8):
            out[8 * n + c] = block[n]


def exact_dot(a, b):
    return lax.dot_general(
        a, b, (((0,), (0,)), ((), ())),
        precision=lax.Precision.HIGHEST, preferred_element_type=F32,
    )


def eliminated(panel, at, width, group):
    done = []
    wide = panel.shape[1] // LANES
    for g in range(0, width, group):
        rows = panel.shape[0]
        row = lax.broadcasted_iota(jnp.int32, (rows, LANES), 0)
        columns = [
            jnp.broadcast_to(panel[:, at + g + t : at + g + t + 1], (rows, LANES))
            for t in range(group)
        ]
        for t in range(group):
            pivot_row = panel[t : t + 1, :]
            pivot = columns[t][t : t + 1, :]
            factor = jnp.where(row > t, columns[t] * (1.0 / pivot), 0.0)
            done.append(pivot_row * jnp.concatenate([lax.rsqrt(pivot)] * wide, axis=1))
            for u in range(t + 1, group):
                columns[u] = columns[u] - factor * columns[u][t : t + 1, :]
            panel = panel - jnp.concatenate([factor] * wide, axis=1) * pivot_row
        panel = panel[group:, :]
    return jnp.concatenate(done, axis=0)


def bases_kernel(meta, arrived, sampled, bases, aug, leaf):
    rank, at = meta[0], meta[1]
    for xh in range(2):
        for k in range(2):
            block = plain(arrived[xh, k])
            leaf[xh, k] = block[:, :32, :] * jnp.exp2(block[:, 32:33, :] - 15.0)
    rows = pl.multiple_of(at // 2 * 8, 8)
    n = 256
    keep = lax.broadcasted_iota(jnp.int32, (1, n), 1) < rank
    own = jnp.concatenate(
        [leaf[at % 2, k, :, pl.ds(rows, 8), :].reshape(64, LANES) for k in range(2)], axis=1
    )
    sampled[...] = own
    full = jnp.concatenate([leaf[:, k].reshape(512, LANES) for k in range(2)], axis=1)
    masked = jnp.where(keep, full, 0.0)
    r = lax.broadcasted_iota(jnp.int32, (n, n), 0)
    c = lax.broadcasted_iota(jnp.int32, (n, n), 1)
    aug[:, :n] = exact_dot(masked, masked) + jnp.where((r == c) & (c >= rank), 1.0, 0.0)
    mine = jnp.where(keep, own, 0.0)
    aug[:, n:] = jnp.concatenate([mine.T, jnp.zeros((n, 64), F32)], axis=1)
    width = 64
    for base in range(0, n, width):
        cut = base // LANES * LANES
        rest = base + width
        panel = eliminated(aug[base:rest, cut:], base - cut, width, 16)
        aug[base:rest, cut:] = panel
        if rest < n:
            low = rest // LANES * LANES
            tail = panel[:, low - cut :]
            update = exact_dot(tail[:, : n - low], tail)
            aug[rest:, low:] = aug[rest:, low:] - update[rest - low :, :]
    bases[...] = aug[:, n : n + 64].T


def ringed(v, stage, shift):
    pairs = []
    for n in range(32):
        xh, core, xl, y = n // 16, n // 8 % 2, n // 4 % 2, n % 4
        x = xh * 2 + xl
        if core == stage:
            y = (y + shift) % 4
        else:
            x = (x + shift) % 4
        pairs.append((n, ((x // 2 * 2 + core) * 2 + x % 2) * 4 + y))
    return lax.ppermute(v, CORES, pairs)


def on_device(front_slab, samples, child_tiles, parent_front, parent_tile, column_tiles, ranks):
    core, xh, xl, y = (lax.axis_index(name) for name in ("core", "xh", "xl", "y"))
    col, x = xl * 4 + y, xh * 2 + xl
    swap = lambda v: lax.ppermute(v, "core", [(0, 1), (1, 0)])
    half = lambda v: jnp.where(core == 0, v[:, :LANES], v[:, LANES:])
    block = jnp.concatenate([half(samples), half(swap(samples))], axis=0)
    child0, slab0 = child_tiles, front_slab[0]
    child1, slab1 = swap(child0), swap(slab0)
    line = jnp.concatenate([block] + [ringed(block, 0, k) for k in (1, 2, 3)], axis=0)
    parts = [line] + [ringed(line, 1, k) for k in (1, 2, 3)]
    held = (parts[1], child1, slab1, column_tiles, parent_front, parent_tile)
    held = lax.optimization_barrier(held)
    parts[1], child1, slab1, column_tiles, parent_front, parent_tile = held
    small = jnp.concatenate([column_tiles.reshape(-1), parent_front[:, 0], parent_tile])
    other = swap(small)
    mine_first = (col // 2) * 8 + (col % 2) * 4 + jnp.arange(4)
    blocks = jnp.concatenate([small[:32] // 2, other[:32] // 2, mine_first])
    dx = (x - (blocks // 16) * 2 - (blocks // 4) % 2) % 4
    dy = (y - blocks) % 4
    first, second = jnp.where(core == 0, dy, dx), jnp.where(core == 0, dx, dy)
    place = (second * 4 + first) * 2 + (blocks // 8 + core) % 2
    odd = jnp.concatenate([small[:32], other[:32]]) % 2
    meta = jnp.concatenate(
        [place[:64] * 2 + odd, small[32:34], other[32:34], small[34:], other[34:]]
        + [place[64:], core[None]]
    ).astype(jnp.int32)
    out = pl.pallas_call(
        products_kernel,
        out_shape=jax.ShapeDtypeStruct((16, 112, LANES), jnp.int16),
        in_specs=[SMEM] + [VMEM] * 5 + [pl.BlockSpec(memory_space=pl.ANY)] * 3,
        out_specs=VMEM,
        scratch_shapes=[
            pltpu.VMEM((8192, LANES), jnp.bfloat16),
            pltpu.VMEM((2, 128, 2048), jnp.bfloat16),
            pltpu.VMEM((512, 1024), jnp.bfloat16),
            pltpu.VMEM((512, 1024), jnp.bfloat16),
            pltpu.SemaphoreType.DMA((10,)),
        ],
        compiler_params=PARAMS,
    )(meta, *parts, child0, child1, slab0, slab1)
    arrived = lax.all_to_all(out, PLANE, 0, 0, tiled=True)
    labels = arrived[:, 108, :8].astype(jnp.int32)
    turned = (core == 1) & (jnp.arange(8) < 4)
    labels = jnp.where(turned, 7 - labels, labels)
    coded, direct = pl.pallas_call(
        combine_kernel,
        out_shape=(
            jax.ShapeDtypeStruct((8, 144, LANES), jnp.int16),
            jax.ShapeDtypeStruct((128, LANES), F32),
        ),
        in_specs=[SMEM, VMEM],
        out_specs=(VMEM, VMEM),
        scratch_shapes=[pltpu.VMEM((8, 128, LANES), F32)] * 4,
        compiler_params=SMALL,
    )(labels, arrived)
    groups = [
        [z * 32 + n for z in (range(8) if n // 8 % 2 == 0 else range(7, -1, -1))]
        for n in range(32)
    ]
    pieces = lax.all_to_all(
        coded, ("z",) + CORES, 0, 0, tiled=True, axis_index_groups=groups
    )
    copies = pl.pallas_call(
        spread_kernel,
        out_shape=jax.ShapeDtypeStruct((32, 40, LANES), jnp.int16),
        in_specs=[VMEM, VMEM],
        out_specs=VMEM,
        compiler_params=SMALL,
    )(pieces, direct)
    leaf = lax.all_to_all(copies, CORES, 0, 0, tiled=True)
    sampled, bases = pl.pallas_call(
        bases_kernel,
        out_shape=(
            jax.ShapeDtypeStruct((64, 256), F32),
            jax.ShapeDtypeStruct((64, 256), F32),
        ),
        in_specs=[SMEM, VMEM],
        out_specs=(VMEM, VMEM),
        scratch_shapes=[
            pltpu.VMEM((256, 384), F32),
            pltpu.VMEM((2, 2, 8, 32, LANES), F32),
        ],
        compiler_params=SMALL,
    )(jnp.stack([ranks[0, 0], col]).astype(jnp.int32), leaf.reshape(2, 2, 8, 40, LANES))
    return sampled[None], bases[None]


def solution(mesh):
    split = Mesh(
        np.asarray(mesh.devices).reshape(8, 2, 2, 2, 4), ("z", "xh", "core", "xl", "y")
    )
    row, col = ("xh", "core"), ("xl", "y")
    in_specs = (
        P("z", row, col),
        P(row + col, None),
        P(("z",) + row + col, None, None),
        P(("z",) + row + col, None),
        P(("z",) + row + col),
        P(("z",) + row + col, None),
        P("z", row),
    )
    out_specs = (P("z", row + col, None), P("z", row + col, None))
    return jax.shard_map(
        on_device, mesh=split, in_specs=in_specs, out_specs=out_specs, check_vma=False
    )
```

```python
import jax
import jax.numpy as jnp
import numpy as np
from jax import lax
from jax.experimental import pallas as pl
from jax.experimental.pallas import tpu as pltpu
from jax.sharding import Mesh, PartitionSpec as P

F32 = jnp.float32
PLANE = ("xh", "xl", "y")
CORES = ("xh", "core", "xl", "y")
VMEM = pl.BlockSpec(memory_space=pltpu.VMEM)
SMEM = pl.BlockSpec(memory_space=pltpu.SMEM)
SMALL = pltpu.CompilerParams(vmem_limit_bytes=16 * 1024 * 1024)
PARAMS = pltpu.CompilerParams(vmem_limit_bytes=50 * 1024 * 1024)
LANES = 128


def exponents(value):
    top = jnp.maximum(jnp.max(jnp.abs(value), axis=1, keepdims=True), 1e-30)
    return jnp.floor(jnp.log2(top)) + 1.0


def coded_as(value, power):
    scaled = jnp.round(value * jnp.exp2(15.0 - power))
    return jnp.clip(scaled, -32767.0, 32767.0).astype(jnp.int32)


def plain(coded):
    return coded.astype(jnp.int32).astype(F32)


def products_kernel(
    meta, part0, part1, part2, part3, child0, child1_in, slab0_in, slab1_in,
    out, omega, child1, slabs, sems,
):
    copies = [
        pltpu.make_async_copy(source, target, sems.at[n])
        for n, (source, target) in enumerate(
            [(child1_in.at[t], child1.at[t]) for t in range(2)]
            + [
                (source.at[pl.ds(128 * t, 128)], slabs.at[pl.ds(512 * o + 128 * t, 128)])
                for o, source in enumerate((slab0_in, slab1_in))
                for t in range(4)
            ]
        )
    ]
    for copy in copies:
        copy.start()
    for n, part in enumerate((part0, part1, part2, part3)):
        omega[2048 * n : 2048 * n + 2048, :] = part[...]
    core = meta[76]
    rows = lax.broadcasted_iota(jnp.int32, (16, LANES), 0)
    lane = lax.broadcasted_iota(jnp.int32, (16, LANES), 1)
    tail = jnp.zeros((16, LANES), jnp.int32)
    for n in range(8):
        tail = jnp.where((rows == 12) & (lane == n), meta[64 + n], tail)

    def kept(tiles, start, tail, first):
        value = jnp.stack(tiles)
        power = exponents(value)
        code = coded_as(value, power).reshape(2, 16, 8, LANES)
        pair = jnp.concatenate([code[0], code[1]], axis=1)
        out[:, pl.ds(pl.multiple_of(start, 16), 16), :] = pair.astype(jnp.int16)
        for n in range(2):
            tail = jnp.where(rows == first + n, power[n].astype(jnp.int32), tail)
        return tail

    for pair in range(2):
        child = (child0, child1)[pair]
        tiles = []
        for t in range(2):
            if pair == 1:
                copies[t].wait()
            acc = jnp.zeros((128, LANES), F32)
            for b in range(0, 16, 2):
                at = 32 * pair + 16 * t + b
                one = omega[pl.ds(pl.multiple_of(meta[at] * 128, 128), 128), :]
                two = omega[pl.ds(pl.multiple_of(meta[at + 1] * 128, 128), 128), :]
                acc += jnp.dot(
                    child[t, :, 128 * b : 128 * b + 256],
                    jnp.concatenate([one, two], axis=0),
                    preferred_element_type=F32,
                )
            tiles.append(acc)
        tail = kept(tiles, 16 * pair, tail, 2 * pair)
    own = jnp.concatenate(
        [omega[pl.ds(pl.multiple_of(meta[72 + b] * 256, 256), 256), :] for b in range(4)], axis=0
    )
    for n in range(2, 10):
        copies[n].wait()
    acc = jnp.dot(slabs[...], own, preferred_element_type=F32).reshape(8, 128, LANES)
    for o in range(2):
        half = core if o == 0 else 1 - core
        for q in (0, 2):
            tiles = [acc[4 * o + q], acc[4 * o + q + 1]]
            tail = kept(tiles, 32 + 32 * half + 8 * q, tail, 4 + 4 * half + q)
    out[:, 96:112, :] = jnp.broadcast_to(tail[None], (16, 16, LANES)).astype(jnp.int16)


def combine_kernel(labels, arrived, coded, direct, *sums):
    for part in sums:
        part[...] = jnp.zeros(part.shape, F32)
    totals = []
    for s in range(16):
        scale = jnp.exp2(plain(arrived[s, 96:112, :]) - 15.0)
        for t in range(4):
            value = plain(arrived[s, 16 * (t // 2) : 16 * (t // 2) + 16, :])
            value = value[8 * (t % 2) : 8 * (t % 2) + 8, :] * scale[t : t + 1, :]
            start = pl.multiple_of(labels[s, 4 + t] * 8, 8)
            sums[t][labels[s, t], pl.ds(start, 8), :] += value
        value = plain(arrived[s, 32:96, :]).reshape(8, 8, LANES) * scale[4:12, None, :]
        if s % 8 == 0:
            totals.append(value)
        else:
            totals[-1] += value
    for p in range(8):
        value = sum(part[p] for part in sums).reshape(16, 8, LANES)
        power = exponents(value)
        coded[p, :128, :] = coded_as(value, power).reshape(128, LANES).astype(jnp.int16)
        coded[p, 128:, :] = power[:, 0, :].astype(jnp.int32).astype(jnp.int16)
    for xh in range(2):
        direct[64 * xh : 64 * xh + 64, :] = totals[xh].reshape(64, LANES)


def spread_kernel(pieces, direct, out):
    total = direct[...].reshape(16, 8, LANES)
    for z in range(8):
        power = plain(pieces[z, 128:, :])
        value = plain(pieces[z, :128, :]).reshape(16, 8, LANES)
        total += value * jnp.exp2(power - 15.0)[:, None, :]
    total = total.reshape(4, 32, LANES)
    power = exponents(total)
    code = coded_as(total, power)
    power = jnp.broadcast_to(power, (4, 8, LANES)).astype(jnp.int32)
    block = jnp.concatenate([code, power], axis=1).astype(jnp.int16)
    for n in range(4):
        for c in range(8):
            out[8 * n + c] = block[n]


def exact_dot(a, b):
    return lax.dot_general(
        a, b, (((0,), (0,)), ((), ())),
        precision=lax.Precision.HIGHEST, preferred_element_type=F32,
    )


def eliminated(panel, at, width, group):
    done = []
    wide = panel.shape[1] // LANES
    for g in range(0, width, group):
        rows = panel.shape[0]
        row = lax.broadcasted_iota(jnp.int32, (rows, LANES), 0)
        columns = [
            jnp.broadcast_to(panel[:, at + g + t : at + g + t + 1], (rows, LANES))
            for t in range(group)
        ]
        for t in range(group):
            pivot_row = panel[t : t + 1, :]
            pivot = columns[t][t : t + 1, :]
            factor = jnp.where(row > t, columns[t] * (1.0 / pivot), 0.0)
            done.append(pivot_row * jnp.concatenate([lax.rsqrt(pivot)] * wide, axis=1))
            for u in range(t + 1, group):
                columns[u] = columns[u] - factor * columns[u][t : t + 1, :]
            panel = panel - jnp.concatenate([factor] * wide, axis=1) * pivot_row
        panel = panel[group:, :]
    return jnp.concatenate(done, axis=0)


def bases_kernel(meta, arrived, sampled, bases, aug, leaf):
    rank, at = meta[0], meta[1]
    for xh in range(2):
        for k in range(2):
            block = plain(arrived[xh, k])
            leaf[xh, k] = block[:, :32, :] * jnp.exp2(block[:, 32:33, :] - 15.0)
    rows = pl.multiple_of(at // 2 * 8, 8)
    n = 256
    keep = lax.broadcasted_iota(jnp.int32, (1, n), 1) < rank
    own = jnp.concatenate(
        [leaf[at % 2, k, :, pl.ds(rows, 8), :].reshape(64, LANES) for k in range(2)], axis=1
    )
    sampled[...] = own
    full = jnp.concatenate([leaf[:, k].reshape(512, LANES) for k in range(2)], axis=1)
    masked = jnp.where(keep, full, 0.0)
    r = lax.broadcasted_iota(jnp.int32, (n, n), 0)
    c = lax.broadcasted_iota(jnp.int32, (n, n), 1)
    aug[:, :n] = exact_dot(masked, masked) + jnp.where((r == c) & (c >= rank), 1.0, 0.0)
    mine = jnp.where(keep, own, 0.0)
    aug[:, n:] = jnp.concatenate([mine.T, jnp.zeros((n, 64), F32)], axis=1)
    width = 64
    for base in range(0, n, width):
        cut = base // LANES * LANES
        rest = base + width
        panel = eliminated(aug[base:rest, cut:], base - cut, width, 16)
        aug[base:rest, cut:] = panel
        if rest < n:
            low = rest // LANES * LANES
            tail = panel[:, low - cut :]
            update = exact_dot(tail[:, : n - low], tail)
            aug[rest:, low:] = aug[rest:, low:] - update[rest - low :, :]
    bases[...] = aug[:, n : n + 64].T


def ringed(v, stage, shift):
    pairs = []
    for n in range(32):
        xh, core, xl, y = n // 16, n // 8 % 2, n // 4 % 2, n % 4
        x = xh * 2 + xl
        if core == stage:
            y = (y + shift) % 4
        else:
            x = (x + shift) % 4
        pairs.append((n, ((x // 2 * 2 + core) * 2 + x % 2) * 4 + y))
    return lax.ppermute(v, CORES, pairs)


def on_device(front_slab, samples, child_tiles, parent_front, parent_tile, column_tiles, ranks):
    core, xh, xl, y = (lax.axis_index(name) for name in ("core", "xh", "xl", "y"))
    col, x = xl * 4 + y, xh * 2 + xl
    swap = lambda v: lax.ppermute(v, "core", [(0, 1), (1, 0)])
    half = lambda v: jnp.where(core == 0, v[:, :LANES], v[:, LANES:])
    block = jnp.concatenate([half(samples), half(swap(samples))], axis=0)
    child0, slab0 = child_tiles, front_slab[0]
    child1, slab1 = swap(child0), swap(slab0)
    line = jnp.concatenate([block] + [ringed(block, 0, k) for k in (1, 2, 3)], axis=0)
    parts = [line] + [ringed(line, 1, k) for k in (1, 2, 3)]
    held = (parts[1], child1, slab1, column_tiles, parent_front, parent_tile)
    held = lax.optimization_barrier(held)
    parts[1], child1, slab1, column_tiles, parent_front, parent_tile = held
    small = jnp.concatenate([column_tiles.reshape(-1), parent_front[:, 0], parent_tile])
    other = swap(small)
    mine_first = (col // 2) * 8 + (col % 2) * 4 + jnp.arange(4)
    blocks = jnp.concatenate([small[:32] // 2, other[:32] // 2, mine_first])
    dx = (x - (blocks // 16) * 2 - (blocks // 4) % 2) % 4
    dy = (y - blocks) % 4
    first, second = jnp.where(core == 0, dy, dx), jnp.where(core == 0, dx, dy)
    place = (second * 4 + first) * 2 + (blocks // 8 + core) % 2
    odd = jnp.concatenate([small[:32], other[:32]]) % 2
    meta = jnp.concatenate(
        [place[:64] * 2 + odd, small[32:34], other[32:34], small[34:], other[34:]]
        + [place[64:], core[None]]
    ).astype(jnp.int32)
    out = pl.pallas_call(
        products_kernel,
        out_shape=jax.ShapeDtypeStruct((16, 112, LANES), jnp.int16),
        in_specs=[SMEM] + [VMEM] * 5 + [pl.BlockSpec(memory_space=pl.ANY)] * 3,
        out_specs=VMEM,
        scratch_shapes=[
            pltpu.VMEM((8192, LANES), jnp.bfloat16),
            pltpu.VMEM((2, 128, 2048), jnp.bfloat16),
            pltpu.VMEM((1024, 1024), jnp.bfloat16),
            pltpu.SemaphoreType.DMA((10,)),
        ],
        compiler_params=PARAMS,
    )(meta, *parts, child0, child1, slab0, slab1)
    arrived = lax.all_to_all(out, PLANE, 0, 0, tiled=True)
    labels = arrived[:, 108, :8].astype(jnp.int32)
    turned = (core == 1) & (jnp.arange(8) < 4)
    labels = jnp.where(turned, 7 - labels, labels)
    coded, direct = pl.pallas_call(
        combine_kernel,
        out_shape=(
            jax.ShapeDtypeStruct((8, 144, LANES), jnp.int16),
            jax.ShapeDtypeStruct((128, LANES), F32),
        ),
        in_specs=[SMEM, VMEM],
        out_specs=(VMEM, VMEM),
        scratch_shapes=[pltpu.VMEM((8, 128, LANES), F32)] * 4,
        compiler_params=SMALL,
    )(labels, arrived)
    groups = [
        [z * 32 + n for z in (range(8) if n // 8 % 2 == 0 else range(7, -1, -1))]
        for n in range(32)
    ]
    pieces = lax.all_to_all(
        coded, ("z",) + CORES, 0, 0, tiled=True, axis_index_groups=groups
    )
    copies = pl.pallas_call(
        spread_kernel,
        out_shape=jax.ShapeDtypeStruct((32, 40, LANES), jnp.int16),
        in_specs=[VMEM, VMEM],
        out_specs=VMEM,
        compiler_params=SMALL,
    )(pieces, direct)
    leaf = lax.all_to_all(copies, CORES, 0, 0, tiled=True)
    sampled, bases = pl.pallas_call(
        bases_kernel,
        out_shape=(
            jax.ShapeDtypeStruct((64, 256), F32),
            jax.ShapeDtypeStruct((64, 256), F32),
        ),
        in_specs=[SMEM, VMEM],
        out_specs=(VMEM, VMEM),
        scratch_shapes=[
            pltpu.VMEM((256, 384), F32),
            pltpu.VMEM((2, 2, 8, 32, LANES), F32),
        ],
        compiler_params=SMALL,
    )(jnp.stack([ranks[0, 0], col]).astype(jnp.int32), leaf.reshape(2, 2, 8, 40, LANES))
    return sampled[None], bases[None]


def solution(mesh):
    split = Mesh(
        np.asarray(mesh.devices).reshape(8, 2, 2, 2, 4), ("z", "xh", "core", "xl", "y")
    )
    row, col = ("xh", "core"), ("xl", "y")
    in_specs = (
        P("z", row, col),
        P(row + col, None),
        P(("z",) + row + col, None, None),
        P(("z",) + row + col, None),
        P(("z",) + row + col),
        P(("z",) + row + col, None),
        P("z", row),
    )
    out_specs = (P("z", row + col, None), P("z", row + col, None))
    return jax.shard_map(
        on_device, mesh=split, in_specs=in_specs, out_specs=out_specs, check_vma=False
    )
```
